512 devices in a mesh: row: 32 (over y, z_hi, core), col: 16 (over x, z_lo).
Axes of the slice: x: 4, y: 8, z: 8 (z_hi: 2, z_lo: 4; z = z_hi * 4 + z_lo), core: 2. Of those that a mesh axis runs over, the one named last changes fastest.
Arguments:
- traces: bfloat16 [2048, 64, 512], P(('row', 'col')), may hold values from -6 to 6
- live_flags: int32 [2048], P(('row', 'col')), may hold values 0 or 1
Outputs:
- correlations: bfloat16 [2048, 2048, 128], P('row', 'col')
The draws below stay inside these ranges and needn't reach their ends.
Inputs may be any that keep to these rules, and one draw needn't show every extreme that they name: `live_flags`: 1 marks a working channel.
All inputs are finite; a program needn't handle non-finite values. No bound on the sum of `live_flags` on one device may be relied on, other than what follows from the above.
Results may differ from the reference program's by a relative error of at most 0.0058.
Values may be sent and summed in bfloat16 or wider, within the bound.
No kernel may reach another device: no remote copies, remote signals or barrier semaphores. Data moves between devices by JAX's collectives and lax.ppermute only.
A program may use at most 64 MiB of HBM per device.

```python
import math
import jax
import jax.numpy as jnp
from jax import lax

C = 2048
F = 256
LAGS = 128
SAMP = 512
NW = 64
N_ROW = 32
N_COL = 16


def plant(array, own_key, low, high):
    shape = array.shape
    spot = [jax.random.randint(jax.random.fold_in(own_key, axis), (), 0, shape[axis]) for axis in range(len(shape))]
    array = array.at[tuple(spot)].set(low)
    longest = shape.index(max(shape))
    spot[longest] = (spot[longest] + 1) % shape[longest]
    return array.at[tuple(spot)].set(high)


def level_of(stream_key, dims, split, low, high):
    def one(position, shards_of):
        draws = jax.random.uniform(jax.random.fold_in(jax.random.fold_in(stream_key, 6), position), (shards_of,), jnp.float32, low / len(split), high / len(split))
        return jnp.repeat(jnp.exp(draws), dims[position] // shards_of).reshape((-1,) + (1,) * (len(dims) - position - 1))

    factor_of = one(*split[0])
    for cut in split[1:]:
        factor_of = factor_of * one(*cut)
    return factor_of


def gaussian(rng, dims, deviation, limit, split=(), kind=jnp.bfloat16):
    factor_of = level_of(rng, dims, split, -0.22, 0.18) if split else 1.0
    array = jax.random.normal(rng, dims, jnp.float32) * deviation * factor_of
    return jnp.minimum(jnp.maximum(array, -limit), limit).astype(kind)


def setup_inputs(seed: int = 0) -> dict:
    splits = jax.random.split(jax.random.key(seed), 3)
    traces = gaussian(splits[0], (C, NW, SAMP), 1.0, 6.0, ((0, 512),))
    live_flags = plant((jax.random.randint(splits[1], (C,), 0, 8) < 7).astype(jnp.int32), jax.random.fold_in(splits[1], 1), 0, 1)
    return dict(traces=traces, live_flags=live_flags)


def make_tables():
    samples = jnp.arange(SAMP, dtype=jnp.int32)
    bins = jnp.arange(F, dtype=jnp.int32)
    phase = samples[:, None] * bins[None, :] % SAMP
    angle = 2.0 * math.pi * phase.astype(jnp.float32) / SAMP
    forward = jnp.concatenate([jnp.cos(angle), -jnp.sin(angle)], axis=1)
    taper = 0.5 - 0.5 * jnp.cos(2.0 * math.pi * samples.astype(jnp.float32) / SAMP)
    near = (jnp.abs(bins[:, None] - bins[None, :]) <= 4).astype(jnp.float32)
    counts = lax.optimization_barrier(jnp.sum(near, axis=0))
    lagval = jnp.arange(LAGS, dtype=jnp.int32) - LAGS // 2
    lphase = bins[:, None] * lagval[None, :] % SAMP
    langle = 2.0 * math.pi * lphase.astype(jnp.float32) / SAMP
    inverse = jnp.concatenate([jnp.cos(langle), -jnp.sin(langle)], axis=0).astype(jnp.bfloat16)
    return (forward, taper, near, counts, inverse)

def whiten(traces, live_flags):
    forward, taper, near, counts, inverse = make_tables()
    chans = traces.shape[0]
    tapered = traces.astype(jnp.float32) * taper
    spectra = jnp.dot(tapered.reshape(-1, SAMP), forward, precision=lax.Precision.HIGHEST)
    real_part = spectra[:, :F]
    imag_part = spectra[:, F:]
    power = real_part * real_part + imag_part * imag_part
    smooth = jnp.dot(power, near, precision=lax.Precision.HIGHEST) / counts
    level = lax.optimization_barrier(jnp.mean(power, axis=1, keepdims=True))
    scale = 1.0 / jnp.sqrt(smooth + 0.05 * level + 1e-06)
    alive = jnp.repeat(live_flags.astype(jnp.float32), NW)[:, None]
    white = jnp.concatenate([real_part * scale, imag_part * scale], axis=1) * alive
    white = white.reshape(chans, NW, 2, F)
    white = jnp.transpose(white, (3, 0, 2, 1)).reshape(F, chans, 2 * NW)
    return white.astype(jnp.bfloat16)

def reference(traces, live_flags):
    forward, taper, near, counts, inverse = make_tables()
    white = whiten(traces, live_flags)
    per_dev = C // (N_ROW * N_COL)
    block = per_dev * N_ROW
    index = jnp.arange(C, dtype=jnp.int32)
    order = (index % block // per_dev * N_COL + index // block) * per_dev + index % per_dev
    second = white[:, order, :].astype(jnp.float32)
    rows = C // N_ROW
    firsts = jnp.transpose(white.reshape(F, N_ROW, rows, 2 * NW), (1, 0, 2, 3))

    def one_block(item):
        first, start = item
        first = first.astype(jnp.float32)
        turned = jnp.concatenate([first[..., NW:], -first[..., :NW]], axis=2)
        cross_re = jnp.einsum('fik,fjk->fij', first, second)
        cross_im = jnp.einsum('fik,fjk->fij', turned, second)
        stacked = (jnp.concatenate([cross_re, cross_im], axis=0) / math.sqrt(NW)).astype(jnp.bfloat16)
        corr = lax.dot_general(stacked, inverse, (((0,), (0,)), ((), ())), preferred_element_type=jnp.float32)
        corr = corr / math.sqrt(F)
        chan_i = start + jnp.arange(rows, dtype=jnp.int32)
        same = chan_i[:, None] == order[None, :]
        corr = jnp.where(same[:, :, None], 0.0, corr)
        return corr.astype(jnp.bfloat16)
    starts = jnp.arange(N_ROW, dtype=jnp.int32) * rows
    result = lax.map(one_block, (firsts, starts))
    return result.reshape(C, C, LAGS)
```

```python
import math

import jax
import jax.numpy as jnp
import numpy as np
from jax import lax
from jax.experimental import pallas as pl
from jax.experimental.pallas import tpu as pltpu
from jax.sharding import PartitionSpec as P

F = 256
LAGS = 128
SAMP = 512
NW = 64
N_Y, N_H, N_C, N_X, N_L = 8, 2, 2, 4, 4
HALF = F // 2
PIECE = HALF * 8
AXES = ("row", "col")


def bf16_parts(table, count):
    parts = []
    rest = table.astype(np.float32)
    for _ in range(count):
        part = rest.astype(jnp.bfloat16)
        parts.append(part)
        rest = rest - part.astype(np.float32)
    return np.stack(parts)


def make_tables():
    samples = np.arange(SAMP)
    bins = np.arange(F)
    angle = 2.0 * math.pi * (bins[:, None] * samples[None, :] % SAMP) / SAMP
    forward = np.concatenate([np.cos(angle), -np.sin(angle)], axis=0)
    taper = 0.5 - 0.5 * np.cos(2.0 * math.pi * samples / SAMP)
    dft = bf16_parts(forward * taper[None, :], 3)
    near = (np.abs(bins[:, None] - bins[None, :]) <= 4).astype(np.float32)
    lags = np.arange(LAGS) - LAGS // 2
    langle = 2.0 * math.pi * (bins[:, None] * lags[None, :] % SAMP) / SAMP
    shift = 1.0 / (math.sqrt(NW) * math.sqrt(F))
    cs = np.cos(langle).astype(np.float32).astype(jnp.bfloat16).astype(np.float32)
    sn = np.sin(langle).astype(np.float32).astype(jnp.bfloat16).astype(np.float32)
    inverse = []
    for half in range(2):
        part = slice(half * HALF, (half + 1) * HALF)
        table = np.concatenate([cs[part], -sn[part]], axis=0) * shift
        inverse.append(table.T.astype(jnp.bfloat16))
    return dft, near, np.stack(inverse)


def whiten_kernel(flags_ref, core_ref, x_ref, dft_ref, near_ref, keep_ref, send_ref, rows_ref):
    x = x_ref[...]
    spectra = None
    for part in (2, 1, 0):
        term = lax.dot_general(
            dft_ref[part], x, (((1,), (1,)), ((), ())), preferred_element_type=jnp.float32
        )
        spectra = term if spectra is None else spectra + term
    re = spectra[:F]
    im = spectra[F:]
    power = re * re + im * im
    bins = lax.broadcasted_iota(jnp.int32, (F, 1), 0)
    counts = jnp.minimum(bins + 4, F - 1) - jnp.maximum(bins - 4, 0) + 1
    smooth = jnp.dot(
        near_ref[...], power, precision=lax.Precision.HIGHEST, preferred_element_type=jnp.float32
    ) / counts.astype(jnp.float32)
    level = jnp.mean(power, axis=0, keepdims=True)
    lane = lax.broadcasted_iota(jnp.int32, (1, 4 * NW), 1) // NW
    alive = jnp.zeros((1, 4 * NW), jnp.float32)
    for ch in range(4):
        alive = jnp.where(lane == ch, flags_ref[ch].astype(jnp.float32), alive)
    scale = lax.rsqrt(smooth + 0.05 * level + 1e-06) * alive
    re = re * scale
    im = im * scale
    low = lax.broadcasted_iota(jnp.int32, (F, 2 * NW), 1) < NW
    for pair in range(2):
        lanes = slice(pair * 2 * NW, (pair + 1) * 2 * NW)
        re2, im2 = re[:, lanes], im[:, lanes]
        rows_ref[pl.ds(2 * pair, F, stride=4), :] = jnp.where(low, re2, pltpu.roll(im2, NW, 1))
        rows_ref[pl.ds(2 * pair + 1, F, stride=4), :] = jnp.where(low, pltpu.roll(re2, NW, 1), im2)
    size = HALF * 4
    core = core_ref[0]
    keep_ref[...] = rows_ref[pl.ds(pl.multiple_of(core * size, size), size), :].astype(jnp.bfloat16)
    send_ref[...] = rows_ref[pl.ds(pl.multiple_of((1 - core) * size, size), size), :].astype(jnp.bfloat16)


def whiten(traces, live_flags, core, dft, near):
    vmem = pl.BlockSpec(memory_space=pltpu.VMEM)
    smem = pl.BlockSpec(memory_space=pltpu.SMEM)
    shape = jax.ShapeDtypeStruct((HALF * 4, 2 * NW), jnp.bfloat16)
    return pl.pallas_call(
        whiten_kernel,
        out_shape=(shape, shape),
        in_specs=[smem, smem, vmem, vmem, vmem],
        out_specs=(vmem, vmem),
        scratch_shapes=[pltpu.VMEM((F * 4, 2 * NW), jnp.float32)],
        name="whiten",
    )(live_flags, core, traces.reshape(4 * NW, SAMP), dft, near)


def merge_kernel(core_ref, keep_ref, got_ref, out_ref):
    keep = keep_ref[...].astype(jnp.float32).reshape(HALF // 2, 8, 2 * NW)
    got = got_ref[...].astype(jnp.float32).reshape(HALF // 2, 8, 2 * NW)
    first = core_ref[0] == 0
    a = jnp.where(first, keep, got)
    b = jnp.where(first, got, keep)
    low = lax.broadcasted_iota(jnp.int32, (HALF // 2, 8, 2 * NW), 1) < 4
    even = jnp.where(low, a, pltpu.roll(b, 4, 1))
    odd = jnp.where(low, pltpu.roll(a, 4, 1), b)
    both = jnp.concatenate([even[:, None], odd[:, None]], axis=1)
    out_ref[...] = both.reshape(PIECE, 2 * NW).astype(jnp.bfloat16)


def merge(core, keep, got):
    vmem = pl.BlockSpec(memory_space=pltpu.VMEM)
    return pl.pallas_call(
        merge_kernel,
        out_shape=jax.ShapeDtypeStruct((PIECE, 2 * NW), jnp.bfloat16),
        in_specs=[pl.BlockSpec(memory_space=pltpu.SMEM), vmem, vmem],
        out_specs=vmem,
        name="merge",
    )(core, keep, got)


N_CHUNK = 4
CHUNK = HALF // N_CHUNK


def cross_kernel(n_first, n_second, where_ref, core_ref, *refs):
    n_in = len(n_first) + len(n_second)
    inputs = refs[:n_in]
    inv_ref, send_ref, own_ref, a_ref, b_ref, s_ref, sem = refs[n_in:]
    copies = []
    for chunk in range(N_CHUNK):
        row = []
        slot = 0
        for index, ref in enumerate(inputs):
            count = (n_first + n_second)[index]
            dst = a_ref if index < len(n_first) else b_ref
            for piece in range(count):
                src = ref.at[piece] if count > 1 else ref
                place = pl.multiple_of(where_ref[slot] * 8, 8)
                bins = pl.ds(chunk * CHUNK, CHUNK)
                copy = pltpu.make_async_copy(
                    src.at[bins], dst.at[bins, pl.ds(place, 8), :], sem.at[chunk, slot]
                )
                copy.start()
                row.append(copy)
                slot += 1
        copies.append(row)
    sign = jnp.where(
        lax.broadcasted_iota(jnp.int32, (128, 2 * NW), 1) < NW, 1.0, -1.0
    ).astype(jnp.bfloat16)
    contract = (((1,), (1,)), ((), ()))

    def one_bin(f, carry):
        a = a_ref[f]
        b = b_ref[f]
        turned = jnp.concatenate([a[:, NW:], a[:, :NW]], axis=1) * sign
        cross_re = lax.dot_general(a, b, contract, preferred_element_type=jnp.float32)
        cross_im = lax.dot_general(turned, b, contract, preferred_element_type=jnp.float32)
        s_ref[pl.ds(f, 128, stride=2 * HALF), :] = cross_re
        s_ref[pl.ds(f + HALF, 128, stride=2 * HALF), :] = cross_im
        return carry

    for chunk in range(N_CHUNK):
        for copy in copies[chunk]:
            copy.wait()
        lax.fori_loop(chunk * CHUNK, (chunk + 1) * CHUNK, one_bin, 0, unroll=4)

    core = core_ref[0]
    table = inv_ref[...]

    def lag_pair(step, which, out_ref):
        piece, half = step // 2, step % 2
        row = piece * 8 + which * 4 + half * 2
        start = pl.multiple_of(row * (2 * HALF), 2 * HALF)
        w0 = s_ref[pl.ds(start, 2 * HALF), :].astype(jnp.bfloat16)
        w1 = s_ref[pl.ds(start + 2 * HALF, 2 * HALF), :].astype(jnp.bfloat16)
        both = jnp.concatenate([w0, w1], axis=1)
        lagged = jnp.dot(table, both, preferred_element_type=jnp.float32)
        i = piece * 4 + half * 2
        out_ref[i] = lagged[:, :128].T.astype(out_ref.dtype)
        out_ref[i + 1] = lagged[:, 128:].T.astype(out_ref.dtype)

    def send_step(step, carry):
        lag_pair(step, 1 - core, send_ref)
        return carry

    def own_step(step, carry):
        lag_pair(step, core, own_ref)
        return carry

    lax.fori_loop(0, 32, send_step, 0, unroll=2)
    lax.fori_loop(0, 32, own_step, 0, unroll=2)


def cross(where, core, firsts, seconds, inverse):
    count = lambda x: 1 if x.ndim == 3 else x.shape[0]
    n_first = tuple(count(x) for x in firsts)
    n_second = tuple(count(x) for x in seconds)
    kernel = lambda *refs: cross_kernel(n_first, n_second, *refs)
    anywhere = pl.BlockSpec(memory_space=pl.ANY)
    vmem = pl.BlockSpec(memory_space=pltpu.VMEM)
    smem = pl.BlockSpec(memory_space=pltpu.SMEM)
    n_in = len(firsts) + len(seconds)
    return pl.pallas_call(
        kernel,
        out_shape=(
            jax.ShapeDtypeStruct((64, 128, LAGS), jnp.bfloat16),
            jax.ShapeDtypeStruct((64, 128, LAGS), jnp.float32),
        ),
        in_specs=[smem, smem] + [anywhere] * n_in + [vmem],
        out_specs=(vmem, vmem),
        scratch_shapes=[
            pltpu.VMEM((HALF, 128, 2 * NW), jnp.bfloat16),
            pltpu.VMEM((HALF, 128, 2 * NW), jnp.bfloat16),
            pltpu.VMEM((128 * 2 * HALF, 128), jnp.float32),
            pltpu.SemaphoreType.DMA((N_CHUNK, 32)),
        ],
        compiler_params=pltpu.CompilerParams(vmem_limit_bytes=56 * 1024 * 1024),
        name="cross",
    )(where, core, *firsts, *seconds, inverse)


def permutation(move):
    pairs = []
    for index in range(N_Y * N_H * N_C * N_X * N_L):
        rest, l = divmod(index, N_L)
        rest, x = divmod(rest, N_X)
        rest, c = divmod(rest, N_C)
        y, h = divmod(rest, N_H)
        y, h, c, x, l = move(y, h, c, x, l)
        pairs.append((index, (((y % N_Y * N_H + h) * N_C + c) * N_X + x % N_X) * N_L + l % N_L))
    return pairs


SWAP_CORE = permutation(lambda y, h, c, x, l: (y, h, 1 - c, x, l))
SWAP_H = permutation(lambda y, h, c, x, l: (y, 1 - h, c, x, l))
STEP_L = [permutation(lambda y, h, c, x, l, d=d: (y, h, c, x, l + d)) for d in range(4)]
Y_UP = permutation(lambda y, h, c, x, l: (y + 1, h, c, x, l))
Y_DOWN = permutation(lambda y, h, c, x, l: (y - 1, h, c, x, l))
X_UP = permutation(lambda y, h, c, x, l: (y, h, c, x + 1, l))
X_DOWN = permutation(lambda y, h, c, x, l: (y, h, c, x - 1, l))


def on_device(traces, live_flags):
    dft, near, inverse = make_tables()
    row = lax.axis_index("row")
    col = lax.axis_index("col")
    y, h, c = row // 4, row // 2 % 2, row % 2
    x, l = col // N_L, col % N_L
    core = c.reshape(1)
    move = lambda value, pairs: lax.ppermute(value, AXES, pairs)
    keep, send = whiten(traces, live_flags, core, jnp.asarray(dft), jnp.asarray(near))
    piece = merge(core, keep, move(send, SWAP_CORE)).reshape(HALF, 8, 2 * NW)

    other = move(piece, SWAP_H)
    near_l = [piece] + [move(piece, STEP_L[d]) for d in (1, 3, 2)]
    y0 = jnp.stack([piece, other])
    up1, down1 = move(y0, Y_UP), move(y0, Y_DOWN)
    x0 = jnp.stack(near_l)
    x_up, x_down = move(x0, X_UP), move(x0, X_DOWN)
    up2, down2 = move(up1, Y_UP), move(down1, Y_DOWN)
    x_far_a, x_far_b = move(x_up[:2], X_UP), move(x_down[2:], X_DOWN)
    up3, down3 = move(up2, Y_UP), move(down2, Y_DOWN)
    far_a, far_b = move(up3[0], Y_UP), move(down3[1], Y_DOWN)

    shifts = (0, 1, 3, 2)
    at_l = [(l - d) % N_L for d in shifts]
    firsts = (x0, x_up, x_down, x_far_a, x_far_b)
    first_at = [x % N_X * N_L + q for q in at_l]
    first_at += [(x - 1) % N_X * N_L + q for q in at_l]
    first_at += [(x + 1) % N_X * N_L + q for q in at_l]
    first_at += [(x + 2) % N_X * N_L + q for q in at_l]
    seconds = (y0, up1, down1, up2, down2, up3, down3, far_a, far_b)
    second_at = []
    for d in (0, -1, 1, -2, 2, -3, 3, 4):
        second_at += [(y + d) % N_Y * N_H + h, (y + d) % N_Y * N_H + 1 - h]
    where = jnp.stack(first_at + second_at).astype(jnp.int32)
    table = lax.dynamic_index_in_dim(jnp.asarray(inverse), c, 0, keepdims=False)
    sent, own = cross(where, core, firsts, seconds, table)
    corr = own + move(sent, SWAP_CORE).astype(jnp.float32)

    rows, cols = corr.shape[:2]
    chan_i = row * rows + jnp.arange(rows, dtype=jnp.int32)
    local_j = jnp.arange(cols, dtype=jnp.int32)
    chan_j = (local_j // 4 * (N_X * N_L) + col) * 4 + local_j % 4
    same = chan_i[:, None] == chan_j[None, :]
    corr = jnp.where(same[:, :, None], 0.0, corr)
    return corr.astype(jnp.bfloat16)


def solution(mesh):
    in_specs = (P(("row", "col"), None, None), P(("row", "col")))
    out_specs = P("row", "col", None)
    return jax.shard_map(
        on_device, mesh=mesh, in_specs=in_specs, out_specs=out_specs, check_vma=False
    )
```

```python
import math

import jax
import jax.numpy as jnp
import numpy as np
from jax import lax
from jax.experimental import pallas as pl
from jax.experimental.pallas import tpu as pltpu
from jax.sharding import PartitionSpec as P

F = 256
LAGS = 128
SAMP = 512
NW = 64
N_Y, N_H, N_C, N_X, N_L = 8, 2, 2, 4, 4
HALF = F // 2
PIECE = HALF * 8
AXES = ("row", "col")


def bf16_parts(table, count):
    parts = []
    rest = table.astype(np.float32)
    for _ in range(count):
        part = rest.astype(jnp.bfloat16)
        parts.append(part)
        rest = rest - part.astype(np.float32)
    return np.stack(parts)


def make_tables():
    samples = np.arange(SAMP)
    bins = np.arange(F)
    angle = 2.0 * math.pi * (bins[:, None] * samples[None, :] % SAMP) / SAMP
    forward = np.concatenate([np.cos(angle), -np.sin(angle)], axis=0)
    taper = 0.5 - 0.5 * np.cos(2.0 * math.pi * samples / SAMP)
    dft = bf16_parts(forward * taper[None, :], 3)
    near = (np.abs(bins[:, None] - bins[None, :]) <= 4).astype(np.float32)
    lags = np.arange(LAGS) - LAGS // 2
    langle = 2.0 * math.pi * (bins[:, None] * lags[None, :] % SAMP) / SAMP
    shift = 1.0 / (math.sqrt(NW) * math.sqrt(F))
    cs = np.cos(langle).astype(np.float32).astype(jnp.bfloat16).astype(np.float32)
    sn = np.sin(langle).astype(np.float32).astype(jnp.bfloat16).astype(np.float32)
    inverse = []
    for half in range(2):
        part = slice(half * HALF, (half + 1) * HALF)
        table = np.concatenate([cs[part], -sn[part]], axis=0) * shift
        inverse.append(table.T.astype(jnp.bfloat16))
    return dft, near, np.stack(inverse)


def whiten_kernel(flags_ref, core_ref, x_ref, dft_ref, near_ref, keep_ref, send_ref, rows_ref):
    x = x_ref[...]
    spectra = None
    for part in (2, 1, 0):
        term = lax.dot_general(
            dft_ref[part], x, (((1,), (1,)), ((), ())), preferred_element_type=jnp.float32
        )
        spectra = term if spectra is None else spectra + term
    re = spectra[:F]
    im = spectra[F:]
    power = re * re + im * im
    bins = lax.broadcasted_iota(jnp.int32, (F, 1), 0)
    counts = jnp.minimum(bins + 4, F - 1) - jnp.maximum(bins - 4, 0) + 1
    smooth = jnp.dot(
        near_ref[...], power, precision=lax.Precision.HIGHEST, preferred_element_type=jnp.float32
    ) / counts.astype(jnp.float32)
    level = jnp.mean(power, axis=0, keepdims=True)
    lane = lax.broadcasted_iota(jnp.int32, (1, 4 * NW), 1) // NW
    alive = jnp.zeros((1, 4 * NW), jnp.float32)
    for ch in range(4):
        alive = jnp.where(lane == ch, flags_ref[ch].astype(jnp.float32), alive)
    scale = lax.rsqrt(smooth + 0.05 * level + 1e-06) * alive
    re = re * scale
    im = im * scale
    low = lax.broadcasted_iota(jnp.int32, (F, 2 * NW), 1) < NW
    for pair in range(2):
        lanes = slice(pair * 2 * NW, (pair + 1) * 2 * NW)
        re2, im2 = re[:, lanes], im[:, lanes]
        rows_ref[pl.ds(2 * pair, F, stride=4), :] = jnp.where(low, re2, pltpu.roll(im2, NW, 1))
        rows_ref[pl.ds(2 * pair + 1, F, stride=4), :] = jnp.where(low, pltpu.roll(re2, NW, 1), im2)
    size = HALF * 4
    core = core_ref[0]
    keep_ref[...] = rows_ref[pl.ds(pl.multiple_of(core * size, size), size), :].astype(jnp.bfloat16)
    send_ref[...] = rows_ref[pl.ds(pl.multiple_of((1 - core) * size, size), size), :].astype(jnp.bfloat16)


def whiten(traces, live_flags, core, dft, near):
    vmem = pl.BlockSpec(memory_space=pltpu.VMEM)
    smem = pl.BlockSpec(memory_space=pltpu.SMEM)
    shape = jax.ShapeDtypeStruct((HALF * 4, 2 * NW), jnp.bfloat16)
    return pl.pallas_call(
        whiten_kernel,
        out_shape=(shape, shape),
        in_specs=[smem, smem, vmem, vmem, vmem],
        out_specs=(vmem, vmem),
        scratch_shapes=[pltpu.VMEM((F * 4, 2 * NW), jnp.float32)],
        name="whiten",
    )(live_flags, core, traces.reshape(4 * NW, SAMP), dft, near)


def merge_kernel(core_ref, keep_ref, got_ref, out_ref):
    keep = keep_ref[...].astype(jnp.float32).reshape(HALF // 2, 8, 2 * NW)
    got = got_ref[...].astype(jnp.float32).reshape(HALF // 2, 8, 2 * NW)
    first = core_ref[0] == 0
    a = jnp.where(first, keep, got)
    b = jnp.where(first, got, keep)
    low = lax.broadcasted_iota(jnp.int32, (HALF // 2, 8, 2 * NW), 1) < 4
    even = jnp.where(low, a, pltpu.roll(b, 4, 1))
    odd = jnp.where(low, pltpu.roll(a, 4, 1), b)
    both = jnp.concatenate([even[:, None], odd[:, None]], axis=1)
    out_ref[...] = both.reshape(PIECE, 2 * NW).astype(jnp.bfloat16)


def merge(core, keep, got):
    vmem = pl.BlockSpec(memory_space=pltpu.VMEM)
    return pl.pallas_call(
        merge_kernel,
        out_shape=jax.ShapeDtypeStruct((PIECE, 2 * NW), jnp.bfloat16),
        in_specs=[pl.BlockSpec(memory_space=pltpu.SMEM), vmem, vmem],
        out_specs=vmem,
        name="merge",
    )(core, keep, got)


N_CHUNK = 4
PITCH = 2 * HALF + 8
CHUNK = HALF // N_CHUNK


def cross_kernel(n_first, n_second, where_ref, core_ref, *refs):
    n_in = len(n_first) + len(n_second)
    inputs = refs[:n_in]
    inv_ref, send_ref, own_ref, a_ref, b_ref, s_ref, sem = refs[n_in:]
    copies = []
    for chunk in range(N_CHUNK):
        row = []
        slot = 0
        for index, ref in enumerate(inputs):
            count = (n_first + n_second)[index]
            dst = a_ref if index < len(n_first) else b_ref
            for piece in range(count):
                src = ref.at[piece] if count > 1 else ref
                place = pl.multiple_of(where_ref[slot] * 8, 8)
                bins = pl.ds(chunk * CHUNK, CHUNK)
                copy = pltpu.make_async_copy(
                    src.at[bins], dst.at[bins, pl.ds(place, 8), :], sem.at[chunk, slot]
                )
                copy.start()
                row.append(copy)
                slot += 1
        copies.append(row)
    sign = jnp.where(
        lax.broadcasted_iota(jnp.int32, (128, 2 * NW), 1) < NW, 1.0, -1.0
    ).astype(jnp.bfloat16)
    contract = (((1,), (1,)), ((), ()))

    def one_bin(f, carry):
        a = a_ref[f]
        b = b_ref[f]
        turned = jnp.concatenate([a[:, NW:], a[:, :NW]], axis=1) * sign
        both = jnp.concatenate([a, turned], axis=0)
        terms = lax.dot_general(both, b, contract, preferred_element_type=jnp.float32)
        s_ref[pl.ds(f, 128, stride=PITCH), :] = terms[:128]
        s_ref[pl.ds(f + HALF, 128, stride=PITCH), :] = terms[128:]
        return carry

    for chunk in range(N_CHUNK):
        for copy in copies[chunk]:
            copy.wait()
        lax.fori_loop(chunk * CHUNK, (chunk + 1) * CHUNK, one_bin, 0, unroll=16)

    core = core_ref[0]
    table = inv_ref[...]

    def lag_pair(step, which, out_ref):
        piece, half = step // 2, step % 2
        row = piece * 8 + which * 4 + half * 2
        start = pl.multiple_of(row * PITCH, 8)
        w0 = s_ref[pl.ds(start, 2 * HALF), :].astype(jnp.bfloat16)
        w1 = s_ref[pl.ds(pl.multiple_of(start + PITCH, 8), 2 * HALF), :].astype(jnp.bfloat16)
        both = jnp.concatenate([w0, w1], axis=1)
        lagged = jnp.dot(table, both, preferred_element_type=jnp.float32)
        i = piece * 4 + half * 2
        out_ref[i] = lagged[:, :128].T.astype(out_ref.dtype)
        out_ref[i + 1] = lagged[:, 128:].T.astype(out_ref.dtype)

    def send_step(step, carry):
        lag_pair(step, 1 - core, send_ref)
        return carry

    def own_step(step, carry):
        lag_pair(step, core, own_ref)
        return carry

    lax.fori_loop(0, 32, send_step, 0, unroll=8)
    lax.fori_loop(0, 32, own_step, 0, unroll=8)


def cross(where, core, firsts, seconds, inverse):
    count = lambda x: 1 if x.ndim == 3 else x.shape[0]
    n_first = tuple(count(x) for x in firsts)
    n_second = tuple(count(x) for x in seconds)
    kernel = lambda *refs: cross_kernel(n_first, n_second, *refs)
    anywhere = pl.BlockSpec(memory_space=pl.ANY)
    vmem = pl.BlockSpec(memory_space=pltpu.VMEM)
    smem = pl.BlockSpec(memory_space=pltpu.SMEM)
    n_in = len(firsts) + len(seconds)
    return pl.pallas_call(
        kernel,
        out_shape=(
            jax.ShapeDtypeStruct((64, 128, LAGS), jnp.bfloat16),
            jax.ShapeDtypeStruct((64, 128, LAGS), jnp.float32),
        ),
        in_specs=[smem, smem] + [anywhere] * n_in + [vmem],
        out_specs=(vmem, vmem),
        scratch_shapes=[
            pltpu.VMEM((HALF, 128, 2 * NW), jnp.bfloat16),
            pltpu.VMEM((HALF, 128, 2 * NW), jnp.bfloat16),
            pltpu.VMEM((128 * PITCH, 128), jnp.float32),
            pltpu.SemaphoreType.DMA((N_CHUNK, 32)),
        ],
        compiler_params=pltpu.CompilerParams(vmem_limit_bytes=56 * 1024 * 1024),
        name="cross",
    )(where, core, *firsts, *seconds, inverse)


def permutation(move):
    pairs = []
    for index in range(N_Y * N_H * N_C * N_X * N_L):
        rest, l = divmod(index, N_L)
        rest, x = divmod(rest, N_X)
        rest, c = divmod(rest, N_C)
        y, h = divmod(rest, N_H)
        y, h, c, x, l = move(y, h, c, x, l)
        pairs.append((index, (((y % N_Y * N_H + h) * N_C + c) * N_X + x % N_X) * N_L + l % N_L))
    return pairs


SWAP_CORE = permutation(lambda y, h, c, x, l: (y, h, 1 - c, x, l))
SWAP_H = permutation(lambda y, h, c, x, l: (y, 1 - h, c, x, l))
STEP_L = [permutation(lambda y, h, c, x, l, d=d: (y, h, c, x, l + d)) for d in range(4)]
Y_UP = permutation(lambda y, h, c, x, l: (y + 1, h, c, x, l))
Y_DOWN = permutation(lambda y, h, c, x, l: (y - 1, h, c, x, l))
X_UP = permutation(lambda y, h, c, x, l: (y, h, c, x + 1, l))
X_DOWN = permutation(lambda y, h, c, x, l: (y, h, c, x - 1, l))


def move(value, pairs):
    return lax.ppermute(value, AXES, pairs)


def correlate(traces, live_flags):
    dft, near, inverse = make_tables()
    row = lax.axis_index("row")
    col = lax.axis_index("col")
    y, h, c = row // 4, row // 2 % 2, row % 2
    x, l = col // N_L, col % N_L
    core = c.reshape(1)
    keep, send = whiten(traces, live_flags, core, jnp.asarray(dft), jnp.asarray(near))
    piece = merge(core, keep, move(send, SWAP_CORE)).reshape(HALF, 8, 2 * NW)

    other = move(piece, SWAP_H)
    up1, down1 = move(piece, Y_UP), move(piece, Y_DOWN)
    l1, l3 = move(piece, STEP_L[1]), move(piece, STEP_L[3])
    up2 = move(jnp.stack([up1, other]), Y_UP)
    down2 = move(jnp.stack([down1, other]), Y_DOWN)
    l2 = move(piece, STEP_L[2])
    x1 = jnp.stack([piece, l1])
    x1_up, x1_down = move(x1, X_UP), move(x1, X_DOWN)
    up3, down3 = move(up2, Y_UP), move(down2, Y_DOWN)
    x2 = jnp.stack([l3, l2])
    x2_up, x2_down = move(x2, X_UP), move(x2, X_DOWN)
    x1_far = move(x1_up, X_UP)
    up4 = move(up3, Y_UP)
    down4 = move(down3[1], Y_DOWN)
    x2_far = move(x2_down, X_DOWN)
    down5 = move(down4, Y_DOWN)

    lead = [l, (l - 1) % N_L]
    rest = [(l - 3) % N_L, (l - 2) % N_L]
    firsts = (x1, x2, x1_up, x2_up, x1_down, x2_down, x1_far, x2_far)
    first_at = []
    for d in (0, -1, 1, 2):
        first_at += [(x + d) % N_X * N_L + q for q in lead + rest]
    seconds = (piece, up1, down1, up2, down2, up3, down3, up4, down4, down5)
    spot = lambda d, mine: (y + d) % N_Y * N_H + (h if mine else 1 - h)
    second_at = [spot(0, True), spot(-1, True), spot(1, True)]
    second_at += [spot(-2, True), spot(-1, False), spot(2, True), spot(1, False)]
    second_at += [spot(-3, True), spot(-2, False), spot(3, True), spot(2, False)]
    second_at += [spot(-4, True), spot(-3, False), spot(3, False), spot(4, False)]
    seconds += (other,)
    second_at += [spot(0, False)]
    where = jnp.stack(first_at + second_at).astype(jnp.int32)
    table = lax.dynamic_index_in_dim(jnp.asarray(inverse), c, 0, keepdims=False)
    sent, own = cross(where, core, firsts, seconds, table)
    corr = own + move(sent, SWAP_CORE).astype(jnp.float32)

    rows, cols = corr.shape[:2]
    chan_i = row * rows + jnp.arange(rows, dtype=jnp.int32)
    local_j = jnp.arange(cols, dtype=jnp.int32)
    chan_j = (local_j // 4 * (N_X * N_L) + col) * 4 + local_j % 4
    same = chan_i[:, None] == chan_j[None, :]
    corr = jnp.where(same[:, :, None], 0.0, corr)
    return corr.astype(jnp.bfloat16)


def solution(mesh):
    in_specs = (P(("row", "col"), None, None), P(("row", "col")))
    out_specs = P("row", "col", None)
    return jax.shard_map(
        correlate, mesh=mesh, in_specs=in_specs, out_specs=out_specs, check_vma=False
    )
```

```python
import math

import jax
import jax.numpy as jnp
import numpy as np
from jax import lax
from jax.experimental import pallas as pl
from jax.experimental.pallas import tpu as pltpu
from jax.sharding import PartitionSpec as P

F = 256
LAGS = 128
SAMP = 512
NW = 64
N_Y, N_H, N_C, N_X, N_L = 8, 2, 2, 4, 4
HALF = F // 2
PIECE = HALF * 8
AXES = ("row", "col")


def bf16_parts(table, count):
    parts = []
    rest = table.astype(np.float32)
    for _ in range(count):
        part = rest.astype(jnp.bfloat16)
        parts.append(part)
        rest = rest - part.astype(np.float32)
    return np.stack(parts)


def make_tables():
    samples = np.arange(SAMP)
    bins = np.arange(F)
    angle = 2.0 * math.pi * (bins[:, None] * samples[None, :] % SAMP) / SAMP
    forward = np.concatenate([np.cos(angle), -np.sin(angle)], axis=0)
    taper = 0.5 - 0.5 * np.cos(2.0 * math.pi * samples / SAMP)
    dft = bf16_parts(forward * taper[None, :], 3)
    near = (np.abs(bins[:, None] - bins[None, :]) <= 4).astype(np.float32)
    lags = np.arange(LAGS) - LAGS // 2
    langle = 2.0 * math.pi * (bins[:, None] * lags[None, :] % SAMP) / SAMP
    shift = 1.0 / (math.sqrt(NW) * math.sqrt(F))
    cs = np.cos(langle).astype(np.float32).astype(jnp.bfloat16).astype(np.float32)
    sn = np.sin(langle).astype(np.float32).astype(jnp.bfloat16).astype(np.float32)
    inverse = []
    for half in range(2):
        part = slice(half * HALF, (half + 1) * HALF)
        table = np.concatenate([cs[part], -sn[part]], axis=0) * shift
        inverse.append(table.T.astype(jnp.bfloat16))
    return dft, near, np.stack(inverse)


def whiten_kernel(flags_ref, x_ref, dft_ref, near_ref, keep_ref, send_ref, rows_ref):
    x = x_ref[...]
    spectra = None
    for part in (2, 1, 0):
        term = lax.dot_general(
            dft_ref[part], x, (((1,), (1,)), ((), ())), preferred_element_type=jnp.float32
        )
        spectra = term if spectra is None else spectra + term
    re = spectra[:F]
    im = spectra[F:]
    power = re * re + im * im
    bins = lax.broadcasted_iota(jnp.int32, (F, 1), 0)
    counts = jnp.minimum(bins + 4, F - 1) - jnp.maximum(bins - 4, 0) + 1
    smooth = jnp.dot(
        near_ref[...], power, precision=lax.Precision.HIGHEST, preferred_element_type=jnp.float32
    ) / counts.astype(jnp.float32)
    level = jnp.mean(power, axis=0, keepdims=True)
    lane = lax.broadcasted_iota(jnp.int32, (1, 4 * NW), 1) // NW
    alive = jnp.zeros((1, 4 * NW), jnp.float32)
    for ch in range(4):
        alive = jnp.where(lane == ch, flags_ref[ch].astype(jnp.float32), alive)
    scale = lax.rsqrt(smooth + 0.05 * level + 1e-06) * alive
    re = re * scale
    im = im * scale
    low = lax.broadcasted_iota(jnp.int32, (F, 2 * NW), 1) < NW
    for pair in range(2):
        lanes = slice(pair * 2 * NW, (pair + 1) * 2 * NW)
        re2, im2 = re[:, lanes], im[:, lanes]
        rows_ref[pl.ds(2 * pair, F, stride=4), :] = jnp.where(low, re2, pltpu.roll(im2, NW, 1))
        rows_ref[pl.ds(2 * pair + 1, F, stride=4), :] = jnp.where(low, pltpu.roll(re2, NW, 1), im2)
    size = HALF * 4
    core = lax.axis_index("row") % N_C
    keep_ref[...] = rows_ref[pl.ds(pl.multiple_of(core * size, size), size), :].astype(jnp.bfloat16)
    send_ref[...] = rows_ref[pl.ds(pl.multiple_of((1 - core) * size, size), size), :].astype(jnp.bfloat16)


def whiten(traces, live_flags, dft, near):
    vmem = pl.BlockSpec(memory_space=pltpu.VMEM)
    smem = pl.BlockSpec(memory_space=pltpu.SMEM)
    shape = jax.ShapeDtypeStruct((HALF * 4, 2 * NW), jnp.bfloat16)
    return pl.pallas_call(
        whiten_kernel,
        out_shape=(shape, shape),
        in_specs=[smem, vmem, vmem, vmem],
        out_specs=(vmem, vmem),
        scratch_shapes=[pltpu.VMEM((F * 4, 2 * NW), jnp.float32)],
        name="whiten",
    )(live_flags, traces.reshape(4 * NW, SAMP), dft, near)


def merge_kernel(keep_ref, got_ref, out_ref):
    keep = keep_ref[...].astype(jnp.float32).reshape(HALF // 2, 8, 2 * NW)
    got = got_ref[...].astype(jnp.float32).reshape(HALF // 2, 8, 2 * NW)
    first = lax.axis_index("row") % N_C == 0
    a = jnp.where(first, keep, got)
    b = jnp.where(first, got, keep)
    low = lax.broadcasted_iota(jnp.int32, (HALF // 2, 8, 2 * NW), 1) < 4
    even = jnp.where(low, a, pltpu.roll(b, 4, 1))
    odd = jnp.where(low, pltpu.roll(a, 4, 1), b)
    both = jnp.concatenate([even[:, None], odd[:, None]], axis=1)
    out_ref[...] = both.reshape(PIECE, 2 * NW).astype(jnp.bfloat16)


def merge(keep, got):
    vmem = pl.BlockSpec(memory_space=pltpu.VMEM)
    return pl.pallas_call(
        merge_kernel,
        out_shape=jax.ShapeDtypeStruct((PIECE, 2 * NW), jnp.bfloat16),
        in_specs=[vmem, vmem],
        out_specs=vmem,
        name="merge",
    )(keep, got)


N_CHUNK = 4
PITCH = 2 * HALF + 8
CHUNK = HALF // N_CHUNK


def placements():
    row, col = lax.axis_index("row"), lax.axis_index("col")
    y, h = row // 4, row // 2 % 2
    x, l = col // N_L, col % N_L
    firsts = []
    for d in (0, -1, 1, 2):
        firsts += [(x + d) % N_X * N_L + (l + q) % N_L for q in (0, 3, 1, 2)]
    spot = lambda d, mine: (y + d) % N_Y * N_H + (h if mine else 1 - h)
    seconds = [spot(0, True), spot(0, False), spot(-1, True)]
    for d in (1, 2, 3):
        seconds += [spot(-d - 1, True), spot(-d, False)]
    for d in (1, 2, 3):
        seconds += [spot(d, True), spot(d, False)]
    seconds += [spot(4, False)]
    return row, col, firsts + seconds


def cross_kernel(n_first, n_second, *refs):
    row, col, where = placements()
    core = row % N_C
    n_in = len(n_first) + len(n_second)
    inputs = refs[:n_in]
    inv_ref, send_ref, own_ref, a_ref, b_ref, s_ref, sem = refs[n_in:]
    copies = []
    for chunk in range(N_CHUNK):
        started = []
        slot = 0
        for index, ref in enumerate(inputs):
            count = (n_first + n_second)[index]
            dst = a_ref if index < len(n_first) else b_ref
            for piece in range(count):
                src = ref.at[piece] if count > 1 else ref
                place = pl.multiple_of(where[slot] * 8, 8)
                bins = pl.ds(chunk * CHUNK, CHUNK)
                copy = pltpu.make_async_copy(
                    src.at[bins], dst.at[bins, pl.ds(place, 8), :], sem.at[chunk, slot]
                )
                copy.start()
                started.append(copy)
                slot += 1
        copies.append(started)
    sign = jnp.where(
        lax.broadcasted_iota(jnp.int32, (128, 2 * NW), 1) < NW, 1.0, -1.0
    ).astype(jnp.bfloat16)
    contract = (((1,), (1,)), ((), ()))

    def one_bin(f, carry):
        a = a_ref[f]
        b = b_ref[f]
        turned = jnp.concatenate([a[:, NW:], a[:, :NW]], axis=1) * sign
        both = jnp.concatenate([a, turned], axis=0)
        terms = lax.dot_general(both, b, contract, preferred_element_type=jnp.float32)
        s_ref[pl.ds(f, 128, stride=PITCH), :] = terms[:128]
        s_ref[pl.ds(f + HALF, 128, stride=PITCH), :] = terms[128:]
        return carry

    for chunk in range(N_CHUNK):
        for copy in copies[chunk]:
            copy.wait()
        lax.fori_loop(chunk * CHUNK, (chunk + 1) * CHUNK, one_bin, 0, unroll=16)

    lane = lax.broadcasted_iota(jnp.int32, (2 * HALF, 128), 1)
    for side in range(N_C):
        for ch in range(4):
            start = pl.multiple_of((col * 8 + side * 4 + ch) * PITCH, 8)
            same = lane == (row - core + side) * 4 + ch
            stacked = s_ref[pl.ds(start, 2 * HALF), :]
            s_ref[pl.ds(start, 2 * HALF), :] = jnp.where(same, 0.0, stacked)
    table = inv_ref[core]

    def lag_pair(step, which, out_ref):
        piece, half = step // 2, step % 2
        row = piece * 8 + which * 4 + half * 2
        start = pl.multiple_of(row * PITCH, 8)
        w0 = s_ref[pl.ds(start, 2 * HALF), :].astype(jnp.bfloat16)
        w1 = s_ref[pl.ds(pl.multiple_of(start + PITCH, 8), 2 * HALF), :].astype(jnp.bfloat16)
        both = jnp.concatenate([w0, w1], axis=1)
        lagged = jnp.dot(table, both, preferred_element_type=jnp.float32)
        i = piece * 4 + half * 2
        out_ref[i] = lagged[:, :128].T.astype(out_ref.dtype)
        out_ref[i + 1] = lagged[:, 128:].T.astype(out_ref.dtype)

    def send_step(step, carry):
        lag_pair(step, 1 - core, send_ref)
        return carry

    def own_step(step, carry):
        lag_pair(step, core, own_ref)
        return carry

    lax.fori_loop(0, 32, send_step, 0, unroll=8)
    lax.fori_loop(0, 32, own_step, 0, unroll=8)


def cross(firsts, seconds, inverse):
    count = lambda x: 1 if x.ndim == 3 else x.shape[0]
    n_first = tuple(count(x) for x in firsts)
    n_second = tuple(count(x) for x in seconds)
    kernel = lambda *refs: cross_kernel(n_first, n_second, *refs)
    anywhere = pl.BlockSpec(memory_space=pl.ANY)
    vmem = pl.BlockSpec(memory_space=pltpu.VMEM)
    n_in = len(firsts) + len(seconds)
    return pl.pallas_call(
        kernel,
        out_shape=(
            pltpu.VMEM((64, 128, LAGS), jnp.bfloat16),
            pltpu.VMEM((64, 128, LAGS), jnp.float32),
        ),
        in_specs=[anywhere] * n_in + [vmem],
        out_specs=(vmem, vmem),
        scratch_shapes=[
            pltpu.VMEM((HALF, 128, 2 * NW), jnp.bfloat16),
            pltpu.VMEM((HALF, 128, 2 * NW), jnp.bfloat16),
            pltpu.VMEM((128 * PITCH, 128), jnp.float32),
            pltpu.SemaphoreType.DMA((N_CHUNK, 32)),
        ],
        compiler_params=pltpu.CompilerParams(vmem_limit_bytes=56 * 1024 * 1024),
        name="cross",
    )(*firsts, *seconds, inverse)


def permutation(move):
    pairs = []
    for index in range(N_Y * N_H * N_C * N_X * N_L):
        rest, l = divmod(index, N_L)
        rest, x = divmod(rest, N_X)
        rest, c = divmod(rest, N_C)
        y, h = divmod(rest, N_H)
        y, h, c, x, l = move(y, h, c, x, l)
        pairs.append((index, (((y % N_Y * N_H + h) * N_C + c) * N_X + x % N_X) * N_L + l % N_L))
    return pairs


SWAP_CORE = permutation(lambda y, h, c, x, l: (y, h, 1 - c, x, l))
SWAP_H = permutation(lambda y, h, c, x, l: (y, 1 - h, c, x, l))
STEP_L = [permutation(lambda y, h, c, x, l, d=d: (y, h, c, x, l + d)) for d in range(4)]
Y_UP = permutation(lambda y, h, c, x, l: (y + 1, h, c, x, l))
Y_DOWN = permutation(lambda y, h, c, x, l: (y - 1, h, c, x, l))
X_UP = permutation(lambda y, h, c, x, l: (y, h, c, x + 1, l))
X_DOWN = permutation(lambda y, h, c, x, l: (y, h, c, x - 1, l))


def move(value, pairs):
    return lax.ppermute(value, AXES, pairs)


def correlate(traces, live_flags):
    dft, near, inverse = make_tables()
    keep, send = whiten(traces, live_flags, jnp.asarray(dft), jnp.asarray(near))
    piece = merge(keep, move(send, SWAP_CORE)).reshape(HALF, 8, 2 * NW)

    other = move(piece, SWAP_H)
    up1 = move(piece, Y_UP)
    l1, l3 = move(piece, STEP_L[1]), move(piece, STEP_L[3])
    up2 = move(jnp.stack([up1, other]), Y_UP)
    down0 = jnp.stack([piece, other])
    down1 = move(down0, Y_DOWN)
    l2 = move(piece, STEP_L[2])
    x1 = jnp.stack([piece, l1])
    x1_up, x1_down = move(x1, X_UP), move(x1, X_DOWN)
    up3, down2 = move(up2, Y_UP), move(down1, Y_DOWN)
    x2 = jnp.stack([l3, l2])
    x2_up, x2_down = move(x2, X_UP), move(x2, X_DOWN)
    x1_far = move(x1_up, X_UP)
    up4, down3 = move(up3, Y_UP), move(down2, Y_DOWN)
    x2_far = move(x2_down, X_DOWN)
    down4 = move(down3[1], Y_DOWN)

    firsts = (x1, x2, x1_up, x2_up, x1_down, x2_down, x1_far, x2_far)
    seconds = (down0, up1, up2, up3, up4, down1, down2, down3, down4)
    sent, own = cross(firsts, seconds, jnp.asarray(inverse))
    got = move(sent, SWAP_CORE)
    return (own + got.astype(jnp.float32)).astype(jnp.bfloat16)


def solution(mesh):
    in_specs = (P(("row", "col"), None, None), P(("row", "col")))
    out_specs = P("row", "col", None)
    return jax.shard_map(
        correlate, mesh=mesh, in_specs=in_specs, out_specs=out_specs, check_vma=False
    )
```

```python
import math

import jax
import jax.numpy as jnp
import numpy as np
from jax import lax
from jax.experimental import pallas as pl
from jax.experimental.pallas import tpu as pltpu
from jax.sharding import PartitionSpec as P

F = 256
LAGS = 128
SAMP = 512
NW = 64
N_Y, N_H, N_C, N_X, N_L = 8, 2, 2, 4, 4
HALF = F // 2
PIECE = HALF * 8
AXES = ("row", "col")


def bf16_parts(table, count):
    parts = []
    rest = table.astype(np.float32)
    for _ in range(count):
        part = rest.astype(jnp.bfloat16)
        parts.append(part)
        rest = rest - part.astype(np.float32)
    return np.stack(parts)


def make_tables():
    samples = np.arange(SAMP)
    bins = np.arange(F)
    angle = 2.0 * math.pi * (bins[:, None] * samples[None, :] % SAMP) / SAMP
    forward = np.concatenate([np.cos(angle), -np.sin(angle)], axis=0)
    taper = 0.5 - 0.5 * np.cos(2.0 * math.pi * samples / SAMP)
    dft = bf16_parts(forward * taper[None, :], 3)
    near = (np.abs(bins[:, None] - bins[None, :]) <= 4).astype(np.float32)
    lags = np.arange(LAGS) - LAGS // 2
    langle = 2.0 * math.pi * (bins[:, None] * lags[None, :] % SAMP) / SAMP
    shift = 1.0 / (math.sqrt(NW) * math.sqrt(F))
    cs = np.cos(langle).astype(np.float32).astype(jnp.bfloat16).astype(np.float32)
    sn = np.sin(langle).astype(np.float32).astype(jnp.bfloat16).astype(np.float32)
    inverse = []
    for half in range(2):
        part = slice(half * HALF, (half + 1) * HALF)
        table = np.concatenate([cs[part], -sn[part]], axis=0) * shift
        inverse.append(table.T.astype(jnp.bfloat16))
    return dft, near, np.stack(inverse)


def whiten_kernel(flags_ref, x_ref, dft_ref, near_ref, keep_ref, send_ref, rows_ref):
    x = x_ref[...]
    spectra = None
    for part in (2, 1, 0):
        term = lax.dot_general(
            dft_ref[part], x, (((1,), (1,)), ((), ())), preferred_element_type=jnp.float32
        )
        spectra = term if spectra is None else spectra + term
    re = spectra[:F]
    im = spectra[F:]
    power = re * re + im * im
    bins = lax.broadcasted_iota(jnp.int32, (F, 1), 0)
    counts = jnp.minimum(bins + 4, F - 1) - jnp.maximum(bins - 4, 0) + 1
    smooth = jnp.dot(
        near_ref[...], power, precision=lax.Precision.HIGHEST, preferred_element_type=jnp.float32
    ) / counts.astype(jnp.float32)
    level = jnp.mean(power, axis=0, keepdims=True)
    lane = lax.broadcasted_iota(jnp.int32, (1, 4 * NW), 1) // NW
    alive = jnp.zeros((1, 4 * NW), jnp.float32)
    for ch in range(4):
        alive = jnp.where(lane == ch, flags_ref[ch].astype(jnp.float32), alive)
    scale = lax.rsqrt(smooth + 0.05 * level + 1e-06) * alive
    re = re * scale
    im = im * scale
    low = lax.broadcasted_iota(jnp.int32, (F, 2 * NW), 1) < NW
    for pair in range(2):
        lanes = slice(pair * 2 * NW, (pair + 1) * 2 * NW)
        re2, im2 = re[:, lanes], im[:, lanes]
        rows_ref[pl.ds(2 * pair, F, stride=4), :] = jnp.where(low, re2, pltpu.roll(im2, NW, 1))
        rows_ref[pl.ds(2 * pair + 1, F, stride=4), :] = jnp.where(low, pltpu.roll(re2, NW, 1), im2)
    size = HALF * 4
    core = lax.axis_index("row") % N_C
    keep_ref[...] = rows_ref[pl.ds(pl.multiple_of(core * size, size), size), :].astype(jnp.bfloat16)
    send_ref[...] = rows_ref[pl.ds(pl.multiple_of((1 - core) * size, size), size), :].astype(jnp.bfloat16)


def whiten(traces, live_flags, dft, near):
    vmem = pl.BlockSpec(memory_space=pltpu.VMEM)
    smem = pl.BlockSpec(memory_space=pltpu.SMEM)
    shape = pltpu.VMEM((HALF * 4, 2 * NW), jnp.bfloat16)
    return pl.pallas_call(
        whiten_kernel,
        out_shape=(shape, shape),
        in_specs=[smem, vmem, vmem, vmem],
        out_specs=(vmem, vmem),
        scratch_shapes=[pltpu.VMEM((F * 4, 2 * NW), jnp.float32)],
        name="whiten",
    )(live_flags, traces.reshape(4 * NW, SAMP), dft, near)


def merge_kernel(keep_ref, got_ref, out_ref):
    keep = keep_ref[...].astype(jnp.float32).reshape(HALF // 2, 8, 2 * NW)
    got = got_ref[...].astype(jnp.float32).reshape(HALF // 2, 8, 2 * NW)
    first = lax.axis_index("row") % N_C == 0
    a = jnp.where(first, keep, got)
    b = jnp.where(first, got, keep)
    low = lax.broadcasted_iota(jnp.int32, (HALF // 2, 8, 2 * NW), 1) < 4
    even = jnp.where(low, a, pltpu.roll(b, 4, 1))
    odd = jnp.where(low, pltpu.roll(a, 4, 1), b)
    both = jnp.concatenate([even[:, None], odd[:, None]], axis=1)
    out_ref[...] = both.reshape(PIECE, 2 * NW).astype(jnp.bfloat16)


def merge(keep, got):
    vmem = pl.BlockSpec(memory_space=pltpu.VMEM)
    return pl.pallas_call(
        merge_kernel,
        out_shape=pltpu.VMEM((PIECE, 2 * NW), jnp.bfloat16),
        in_specs=[vmem, vmem],
        out_specs=vmem,
        name="merge",
    )(in_vmem(keep), in_vmem(got))


N_CHUNK = 4
PITCH = 2 * HALF + 8
CHUNK = HALF // N_CHUNK


def placements():
    row, col = lax.axis_index("row"), lax.axis_index("col")
    y, h = row // 4, row // 2 % 2
    x, l = col // N_L, col % N_L
    firsts = []
    for d in (0, -1, 1, 2):
        firsts += [(x + d) % N_X * N_L + (l + q) % N_L for q in (0, 3, 1, 2)]
    spot = lambda d, mine: (y + d) % N_Y * N_H + (h if mine else 1 - h)
    seconds = [spot(0, True), spot(0, False), spot(-1, True), spot(1, True)]
    for d in (1, 2):
        seconds += [spot(-d - 1, True), spot(-d, False), spot(d + 1, True), spot(d, False)]
    seconds += [spot(-4, True), spot(-3, False), spot(3, False), spot(4, False)]
    return row, col, firsts + seconds


def cross_kernel(n_first, n_second, *refs):
    row, col, where = placements()
    core = row % N_C
    n_in = len(n_first) + len(n_second)
    inputs = refs[:n_in]
    inv_ref, send_ref, own_ref, a_ref, b_ref, s_ref, sem = refs[n_in:]
    copies = []
    for chunk in range(N_CHUNK):
        started = []
        slot = 0
        for index, ref in enumerate(inputs):
            count = (n_first + n_second)[index]
            dst = a_ref if index < len(n_first) else b_ref
            for piece in range(count):
                src = ref.at[piece] if count > 1 else ref
                place = pl.multiple_of(where[slot] * 8, 8)
                bins = pl.ds(chunk * CHUNK, CHUNK)
                copy = pltpu.make_async_copy(
                    src.at[bins], dst.at[bins, pl.ds(place, 8), :], sem.at[chunk, slot]
                )
                copy.start()
                started.append(copy)
                slot += 1
        copies.append(started)
    sign = jnp.where(
        lax.broadcasted_iota(jnp.int32, (128, 2 * NW), 1) < NW, 1.0, -1.0
    ).astype(jnp.bfloat16)
    contract = (((1,), (1,)), ((), ()))

    def one_bin(f, carry):
        a = a_ref[f]
        b = b_ref[f]
        turned = jnp.concatenate([a[:, NW:], a[:, :NW]], axis=1) * sign
        both = jnp.concatenate([a, turned], axis=0)
        terms = lax.dot_general(both, b, contract, preferred_element_type=jnp.float32)
        s_ref[pl.ds(f, 128, stride=PITCH), :] = terms[:128]
        s_ref[pl.ds(f + HALF, 128, stride=PITCH), :] = terms[128:]
        return carry

    for chunk in range(N_CHUNK):
        for copy in copies[chunk]:
            copy.wait()
        lax.fori_loop(chunk * CHUNK, (chunk + 1) * CHUNK, one_bin, 0, unroll=16)

    lane = lax.broadcasted_iota(jnp.int32, (2 * HALF, 128), 1)
    for side in range(N_C):
        for ch in range(4):
            start = pl.multiple_of((col * 8 + side * 4 + ch) * PITCH, 8)
            same = lane == (row - core + side) * 4 + ch
            stacked = s_ref[pl.ds(start, 2 * HALF), :]
            s_ref[pl.ds(start, 2 * HALF), :] = jnp.where(same, 0.0, stacked)
    table = inv_ref[core]

    def lag_pair(step, which, out_ref):
        piece, half = step // 2, step % 2
        row = piece * 8 + which * 4 + half * 2
        start = pl.multiple_of(row * PITCH, 8)
        w0 = s_ref[pl.ds(start, 2 * HALF), :].astype(jnp.bfloat16)
        w1 = s_ref[pl.ds(pl.multiple_of(start + PITCH, 8), 2 * HALF), :].astype(jnp.bfloat16)
        both = jnp.concatenate([w0, w1], axis=1)
        lagged = jnp.dot(table, both, preferred_element_type=jnp.float32)
        i = piece * 4 + half * 2
        out_ref[i] = lagged[:, :128].T.astype(out_ref.dtype)
        out_ref[i + 1] = lagged[:, 128:].T.astype(out_ref.dtype)

    def send_step(step, carry):
        lag_pair(step, 1 - core, send_ref)
        return carry

    def own_step(step, carry):
        lag_pair(step, core, own_ref)
        return carry

    lax.fori_loop(0, 32, send_step, 0, unroll=8)
    lax.fori_loop(0, 32, own_step, 0, unroll=8)


def cross(firsts, seconds, inverse):
    count = lambda x: 1 if x.ndim == 3 else x.shape[0]
    n_first = tuple(count(x) for x in firsts)
    n_second = tuple(count(x) for x in seconds)
    kernel = lambda *refs: cross_kernel(n_first, n_second, *refs)
    vmem = pl.BlockSpec(memory_space=pltpu.VMEM)
    n_in = len(firsts) + len(seconds)
    return pl.pallas_call(
        kernel,
        out_shape=(
            pltpu.VMEM((64, 128, LAGS), jnp.bfloat16),
            pltpu.VMEM((64, 128, LAGS), jnp.float32),
        ),
        in_specs=[vmem] * (n_in + 1),
        out_specs=(vmem, vmem),
        scratch_shapes=[
            pltpu.VMEM((HALF, 128, 2 * NW), jnp.bfloat16),
            pltpu.VMEM((HALF, 128, 2 * NW), jnp.bfloat16),
            pltpu.VMEM((128 * PITCH, 128), jnp.float32),
            pltpu.SemaphoreType.DMA((N_CHUNK, 32)),
        ],
        compiler_params=pltpu.CompilerParams(vmem_limit_bytes=32 * 1024 * 1024),
        name="cross",
    )(*[in_vmem(value) for value in (*firsts, *seconds)], inverse)


def permutation(move):
    pairs = []
    for index in range(N_Y * N_H * N_C * N_X * N_L):
        rest, l = divmod(index, N_L)
        rest, x = divmod(rest, N_X)
        rest, c = divmod(rest, N_C)
        y, h = divmod(rest, N_H)
        y, h, c, x, l = move(y, h, c, x, l)
        pairs.append((index, (((y % N_Y * N_H + h) * N_C + c) * N_X + x % N_X) * N_L + l % N_L))
    return pairs


SWAP_CORE = permutation(lambda y, h, c, x, l: (y, h, 1 - c, x, l))
SWAP_H = permutation(lambda y, h, c, x, l: (y, 1 - h, c, x, l))
STEP_L = [permutation(lambda y, h, c, x, l, d=d: (y, h, c, x, l + d)) for d in range(4)]
Y_UP = permutation(lambda y, h, c, x, l: (y + 1, h, c, x, l))
Y_DOWN = permutation(lambda y, h, c, x, l: (y - 1, h, c, x, l))
X_UP = permutation(lambda y, h, c, x, l: (y, h, c, x + 1, l))
X_DOWN = permutation(lambda y, h, c, x, l: (y, h, c, x - 1, l))


def in_vmem(value):
    return pltpu.with_memory_space_constraint(value, pltpu.VMEM)


def move(value, pairs):
    return lax.ppermute(value, AXES, pairs)


def correlate(traces, live_flags):
    dft, near, inverse = make_tables()
    keep, send = whiten(traces, live_flags, jnp.asarray(dft), jnp.asarray(near))
    piece = merge(keep, move(send, SWAP_CORE)).reshape(HALF, 8, 2 * NW)

    other = move(piece, SWAP_H)
    up1, down1 = move(piece, Y_UP), move(piece, Y_DOWN)
    l1, l3 = move(piece, STEP_L[1]), move(piece, STEP_L[3])
    up2 = move(jnp.stack([up1, other]), Y_UP)
    down2 = move(jnp.stack([down1, other]), Y_DOWN)
    l2 = move(piece, STEP_L[2])
    x1 = jnp.stack([piece, l1])
    x1_up, x1_down = move(x1, X_UP), move(x1, X_DOWN)
    up3, down3 = move(up2, Y_UP), move(down2, Y_DOWN)
    x2 = jnp.stack([l3, l2])
    x2_up, x2_down = move(x2, X_UP), move(x2, X_DOWN)
    x1_far = move(x1_up, X_UP)
    up4 = move(up3, Y_UP)
    down4 = move(down3[1], Y_DOWN)
    x2_far = move(x2_down, X_DOWN)
    down5 = move(down4, Y_DOWN)

    firsts = (x1, x2, x1_up, x2_up, x1_down, x2_down, x1_far, x2_far)
    seconds = (piece, other, up1, down1, up2, down2, up3, down3, up4, down4, down5)
    sent, own = cross(firsts, seconds, jnp.asarray(inverse))
    got = move(sent, SWAP_CORE)
    return (own + got.astype(jnp.float32)).astype(jnp.bfloat16)


def solution(mesh):
    in_specs = (P(("row", "col"), None, None), P(("row", "col")))
    out_specs = P("row", "col", None)
    return jax.shard_map(
        correlate, mesh=mesh, in_specs=in_specs, out_specs=out_specs, check_vma=False
    )
```

```python
import math

import jax
import jax.numpy as jnp
import numpy as np
from jax import lax
from jax.experimental import pallas as pl
from jax.experimental.pallas import tpu as pltpu
from jax.sharding import PartitionSpec as P

F = 256
LAGS = 128
SAMP = 512
NW = 64
N_Y, N_H, N_C, N_X, N_L = 8, 2, 2, 4, 4
HALF = F // 2
PIECE = HALF * 8
AXES = ("row", "col")


def bf16_parts(table, count):
    parts = []
    rest = table.astype(np.float32)
    for _ in range(count):
        part = rest.astype(jnp.bfloat16)
        parts.append(part)
        rest = rest - part.astype(np.float32)
    return np.stack(parts)


def make_tables():
    samples = np.arange(SAMP)
    bins = np.arange(F)
    angle = 2.0 * math.pi * (bins[:, None] * samples[None, :] % SAMP) / SAMP
    forward = np.concatenate([np.cos(angle), -np.sin(angle)], axis=0)
    taper = 0.5 - 0.5 * np.cos(2.0 * math.pi * samples / SAMP)
    dft = bf16_parts(forward * taper[None, :], 3)
    near = (np.abs(bins[:, None] - bins[None, :]) <= 4).astype(np.float32)
    lags = np.arange(LAGS) - LAGS // 2
    langle = 2.0 * math.pi * (bins[:, None] * lags[None, :] % SAMP) / SAMP
    shift = 1.0 / (math.sqrt(NW) * math.sqrt(F))
    cs = np.cos(langle).astype(np.float32).astype(jnp.bfloat16).astype(np.float32)
    sn = np.sin(langle).astype(np.float32).astype(jnp.bfloat16).astype(np.float32)
    inverse = []
    for half in range(2):
        part = slice(half * HALF, (half + 1) * HALF)
        table = np.concatenate([cs[part], -sn[part]], axis=0) * shift
        inverse.append(table.T.astype(jnp.bfloat16))
    return dft, near, np.stack(inverse)


def whiten_kernel(flags_ref, x_ref, dft_ref, near_ref, keep_ref, send_ref, rows_ref):
    x = x_ref[...]
    spectra = None
    for part in (2, 1, 0):
        term = lax.dot_general(
            dft_ref[part], x, (((1,), (1,)), ((), ())), preferred_element_type=jnp.float32
        )
        spectra = term if spectra is None else spectra + term
    re = spectra[:F]
    im = spectra[F:]
    power = re * re + im * im
    bins = lax.broadcasted_iota(jnp.int32, (F, 1), 0)
    counts = jnp.minimum(bins + 4, F - 1) - jnp.maximum(bins - 4, 0) + 1
    smooth = jnp.dot(
        near_ref[...], power, precision=lax.Precision.HIGHEST, preferred_element_type=jnp.float32
    ) / counts.astype(jnp.float32)
    level = jnp.mean(power, axis=0, keepdims=True)
    lane = lax.broadcasted_iota(jnp.int32, (1, 4 * NW), 1) // NW
    alive = jnp.zeros((1, 4 * NW), jnp.float32)
    for ch in range(4):
        alive = jnp.where(lane == ch, flags_ref[ch].astype(jnp.float32), alive)
    scale = lax.rsqrt(smooth + 0.05 * level + 1e-06) * alive
    re = re * scale
    im = im * scale
    low = lax.broadcasted_iota(jnp.int32, (F, 2 * NW), 1) < NW
    for pair in range(2):
        lanes = slice(pair * 2 * NW, (pair + 1) * 2 * NW)
        re2, im2 = re[:, lanes], im[:, lanes]
        rows_ref[pl.ds(2 * pair, F, stride=4), :] = jnp.where(low, re2, pltpu.roll(im2, NW, 1))
        rows_ref[pl.ds(2 * pair + 1, F, stride=4), :] = jnp.where(low, pltpu.roll(re2, NW, 1), im2)
    size = HALF * 4
    core = lax.axis_index("row") % N_C
    keep_ref[...] = rows_ref[pl.ds(pl.multiple_of(core * size, size), size), :].astype(jnp.bfloat16)
    send_ref[...] = rows_ref[pl.ds(pl.multiple_of((1 - core) * size, size), size), :].astype(jnp.bfloat16)


def whiten(traces, live_flags, dft, near):
    vmem = pl.BlockSpec(memory_space=pltpu.VMEM)
    smem = pl.BlockSpec(memory_space=pltpu.SMEM)
    shape = pltpu.VMEM((HALF * 4, 2 * NW), jnp.bfloat16)
    return pl.pallas_call(
        whiten_kernel,
        out_shape=(shape, shape),
        in_specs=[smem, vmem, vmem, vmem],
        out_specs=(vmem, vmem),
        scratch_shapes=[pltpu.VMEM((F * 4, 2 * NW), jnp.float32)],
        name="whiten",
    )(live_flags, traces.reshape(4 * NW, SAMP), dft, near)


def merge_kernel(keep_ref, got_ref, out_ref):
    keep = keep_ref[...].astype(jnp.float32).reshape(HALF // 2, 8, 2 * NW)
    got = got_ref[...].astype(jnp.float32).reshape(HALF // 2, 8, 2 * NW)
    first = lax.axis_index("row") % N_C == 0
    a = jnp.where(first, keep, got)
    b = jnp.where(first, got, keep)
    low = lax.broadcasted_iota(jnp.int32, (HALF // 2, 8, 2 * NW), 1) < 4
    even = jnp.where(low, a, pltpu.roll(b, 4, 1))
    odd = jnp.where(low, pltpu.roll(a, 4, 1), b)
    both = jnp.concatenate([even[:, None], odd[:, None]], axis=1)
    out_ref[...] = both.reshape(PIECE, 2 * NW).astype(jnp.bfloat16)


def merge(keep, got):
    vmem = pl.BlockSpec(memory_space=pltpu.VMEM)
    return pl.pallas_call(
        merge_kernel,
        out_shape=pltpu.VMEM((PIECE, 2 * NW), jnp.bfloat16),
        in_specs=[vmem, vmem],
        out_specs=vmem,
        name="merge",
    )(in_vmem(keep), in_vmem(got))


PITCH = 2 * HALF + 8


def placements():
    row, col = lax.axis_index("row"), lax.axis_index("col")
    y, h = row // 4, row // 2 % 2
    x, l = col // N_L, col % N_L
    firsts = []
    for d in (0, -1, 1, 2):
        firsts += [(x + d) % N_X * N_L + (l + q) % N_L for q in (0, 3, 1, 2)]
    spot = lambda d, mine: (y + d) % N_Y * N_H + (h if mine else 1 - h)
    seconds = [spot(0, True), spot(0, False), spot(-1, True), spot(1, True)]
    for d in (1, 2):
        seconds += [spot(-d - 1, True), spot(-d, False), spot(d + 1, True), spot(d, False)]
    seconds += [spot(-4, True), spot(-3, False), spot(3, False), spot(4, False)]
    return row, col, firsts + seconds


def cross_kernel(n_first, *refs):
    firsts, seconds = refs[:n_first], refs[n_first:-5]
    inv_ref, send_ref, own_ref, s_ref, place_ref = refs[-5:]
    row, _, where = placements()
    core = row % N_C
    for slot in range(16):
        place_ref[slot] = where[slot]
    sign = jnp.where(
        lax.broadcasted_iota(jnp.int32, (128, 2 * NW), 1) < NW, 1.0, -1.0
    ).astype(jnp.bfloat16)
    contract = (((1,), (1,)), ((), ()))

    def gather(blocks, f):
        parts = []
        for ref in blocks:
            parts += [ref[f]] if len(ref.shape) == 3 else [ref[n, f] for n in range(ref.shape[0])]
        return jnp.concatenate(parts, axis=0)

    def one_bin(f, carry):
        a = gather(firsts, f)
        b = gather(seconds, f)
        turned = jnp.concatenate([a[:, NW:], a[:, :NW]], axis=1) * sign
        both = jnp.concatenate([a, turned], axis=0)
        terms = lax.dot_general(both, b, contract, preferred_element_type=jnp.float32)
        s_ref[pl.ds(f, 128, stride=PITCH), :] = terms[:128]
        s_ref[pl.ds(f + HALF, 128, stride=PITCH), :] = terms[128:]
        return carry

    lax.fori_loop(0, HALF, one_bin, 0, unroll=UNROLL)

    lane = lax.broadcasted_iota(jnp.int32, (2 * HALF, 128), 1)
    for slot in range(8):
        rows = pl.ds(slot * PITCH, 2 * HALF)
        s_ref[rows, :] = jnp.where(lane == slot, 0.0, s_ref[rows, :])
    table = inv_ref[core]
    spots = [pl.ds(pl.multiple_of(place * 8, 8), 8) for place in where[16:]]

    def lag_pair(step, which, out_ref):
        piece, half = step // 2, step % 2
        start = pl.multiple_of((piece * 8 + which * 4 + half * 2) * PITCH, 8)
        w0 = s_ref[pl.ds(start, 2 * HALF), :].astype(jnp.bfloat16)
        w1 = s_ref[pl.ds(pl.multiple_of(start + PITCH, 8), 2 * HALF), :].astype(jnp.bfloat16)
        lagged = jnp.dot(table, jnp.concatenate([w0, w1], axis=1), preferred_element_type=jnp.float32)
        i = place_ref[piece] * 4 + half * 2
        for n in range(2):
            block = lagged[:, n * 128 : (n + 1) * 128].T
            for slot in range(16):
                out_ref[i + n, spots[slot], :] = block[slot * 8 : slot * 8 + 8].astype(out_ref.dtype)

    def send_step(step, carry):
        lag_pair(step, 1 - core, send_ref)
        return carry

    def own_step(step, carry):
        lag_pair(step, core, own_ref)
        return carry

    lax.fori_loop(0, 32, send_step, 0, unroll=16)
    lax.fori_loop(0, 32, own_step, 0, unroll=16)


UNROLL = 16


def cross(firsts, seconds, inverse):
    kernel = lambda *refs: cross_kernel(len(firsts), *refs)
    vmem = pl.BlockSpec(memory_space=pltpu.VMEM)
    return pl.pallas_call(
        kernel,
        out_shape=(
            pltpu.VMEM((64, 128, LAGS), jnp.bfloat16),
            pltpu.VMEM((64, 128, LAGS), jnp.float32),
        ),
        in_specs=[vmem] * (len(firsts) + len(seconds) + 1),
        out_specs=(vmem, vmem),
        scratch_shapes=[
            pltpu.VMEM((128 * PITCH, 128), jnp.float32),
            pltpu.SMEM((16,), jnp.int32),
        ],
        compiler_params=pltpu.CompilerParams(vmem_limit_bytes=32 * 1024 * 1024),
        name="cross",
    )(*[in_vmem(value) for value in (*firsts, *seconds)], inverse)


def permutation(move):
    pairs = []
    for index in range(N_Y * N_H * N_C * N_X * N_L):
        rest, l = divmod(index, N_L)
        rest, x = divmod(rest, N_X)
        rest, c = divmod(rest, N_C)
        y, h = divmod(rest, N_H)
        y, h, c, x, l = move(y, h, c, x, l)
        pairs.append((index, (((y % N_Y * N_H + h) * N_C + c) * N_X + x % N_X) * N_L + l % N_L))
    return pairs


SWAP_CORE = permutation(lambda y, h, c, x, l: (y, h, 1 - c, x, l))
SWAP_H = permutation(lambda y, h, c, x, l: (y, 1 - h, c, x, l))
STEP_L = [permutation(lambda y, h, c, x, l, d=d: (y, h, c, x, l + d)) for d in range(4)]
Y_UP = permutation(lambda y, h, c, x, l: (y + 1, h, c, x, l))
Y_DOWN = permutation(lambda y, h, c, x, l: (y - 1, h, c, x, l))
X_UP = permutation(lambda y, h, c, x, l: (y, h, c, x + 1, l))
X_DOWN = permutation(lambda y, h, c, x, l: (y, h, c, x - 1, l))


def in_vmem(value):
    return pltpu.with_memory_space_constraint(value, pltpu.VMEM)


def move(value, pairs):
    return lax.ppermute(value, AXES, pairs)


def correlate(traces, live_flags):
    dft, near, inverse = make_tables()
    keep, send = whiten(traces, live_flags, jnp.asarray(dft), jnp.asarray(near))
    piece = merge(keep, move(send, SWAP_CORE)).reshape(HALF, 8, 2 * NW)

    other = move(piece, SWAP_H)
    up1, down1 = move(piece, Y_UP), move(piece, Y_DOWN)
    l1, l3 = move(piece, STEP_L[1]), move(piece, STEP_L[3])
    up2 = move(jnp.stack([up1, other]), Y_UP)
    down2 = move(jnp.stack([down1, other]), Y_DOWN)
    l2 = move(piece, STEP_L[2])
    x1 = jnp.stack([piece, l1])
    x1_up, x1_down = move(x1, X_UP), move(x1, X_DOWN)
    up3, down3 = move(up2, Y_UP), move(down2, Y_DOWN)
    x2 = jnp.stack([l3, l2])
    x2_up, x2_down = move(x2, X_UP), move(x2, X_DOWN)
    x1_far = move(x1_up, X_UP)
    up4 = move(up3, Y_UP)
    down4 = move(down3[1], Y_DOWN)
    x2_far = move(x2_down, X_DOWN)
    down5 = move(down4, Y_DOWN)

    firsts = (x1, x2, x1_up, x2_up, x1_down, x2_down, x1_far, x2_far)
    seconds = (piece, other, up1, down1, up2, down2, up3, down3, up4, down4, down5)
    sent, own = cross(firsts, seconds, jnp.asarray(inverse))
    got = move(sent, SWAP_CORE)
    return (own + got.astype(jnp.float32)).astype(jnp.bfloat16)


def solution(mesh):
    in_specs = (P(("row", "col"), None, None), P(("row", "col")))
    out_specs = P("row", "col", None)
    return jax.shard_map(
        correlate, mesh=mesh, in_specs=in_specs, out_specs=out_specs, check_vma=False
    )
```

```python
import math

import jax
import jax.numpy as jnp
import numpy as np
from jax import lax
from jax.experimental import pallas as pl
from jax.experimental.pallas import tpu as pltpu
from jax.sharding import PartitionSpec as P

F = 256
LAGS = 128
SAMP = 512
NW = 64
N_Y, N_H, N_C, N_X, N_L = 8, 2, 2, 4, 4
HALF = F // 2
PIECE = HALF * 8
AXES = ("row", "col")


def bf16_parts(table, count):
    parts = []
    rest = table.astype(np.float32)
    for _ in range(count):
        part = rest.astype(jnp.bfloat16)
        parts.append(part)
        rest = rest - part.astype(np.float32)
    return np.stack(parts)


def make_tables():
    samples = np.arange(SAMP)
    bins = np.arange(F)
    angle = 2.0 * math.pi * (bins[:, None] * samples[None, :] % SAMP) / SAMP
    forward = np.concatenate([np.cos(angle), -np.sin(angle)], axis=0)
    taper = 0.5 - 0.5 * np.cos(2.0 * math.pi * samples / SAMP)
    dft = bf16_parts(forward * taper[None, :], 3)
    near = (np.abs(bins[:, None] - bins[None, :]) <= 4).astype(np.float32)
    lags = np.arange(LAGS) - LAGS // 2
    langle = 2.0 * math.pi * (bins[:, None] * lags[None, :] % SAMP) / SAMP
    shift = 1.0 / (math.sqrt(NW) * math.sqrt(F))
    cs = np.cos(langle).astype(np.float32).astype(jnp.bfloat16).astype(np.float32)
    sn = np.sin(langle).astype(np.float32).astype(jnp.bfloat16).astype(np.float32)
    inverse = []
    for half in range(2):
        part = slice(half * HALF, (half + 1) * HALF)
        table = np.concatenate([cs[part], -sn[part]], axis=0) * shift
        inverse.append(table.T.astype(jnp.bfloat16))
    return dft, near, np.stack(inverse)


def whiten_kernel(flags_ref, x_ref, dft_ref, near_ref, keep_ref, send_ref, rows_ref):
    x = x_ref[...]
    spectra = None
    for part in (2, 1, 0):
        term = lax.dot_general(
            dft_ref[part], x, (((1,), (1,)), ((), ())), preferred_element_type=jnp.float32
        )
        spectra = term if spectra is None else spectra + term
    re = spectra[:F]
    im = spectra[F:]
    power = re * re + im * im
    bins = lax.broadcasted_iota(jnp.int32, (F, 1), 0)
    counts = jnp.minimum(bins + 4, F - 1) - jnp.maximum(bins - 4, 0) + 1
    smooth = jnp.dot(
        near_ref[...], power, precision=lax.Precision.HIGHEST, preferred_element_type=jnp.float32
    ) / counts.astype(jnp.float32)
    level = jnp.mean(power, axis=0, keepdims=True)
    lane = lax.broadcasted_iota(jnp.int32, (1, 4 * NW), 1) // NW
    alive = jnp.zeros((1, 4 * NW), jnp.float32)
    for ch in range(4):
        alive = jnp.where(lane == ch, flags_ref[ch].astype(jnp.float32), alive)
    scale = lax.rsqrt(smooth + 0.05 * level + 1e-06) * alive
    re = re * scale
    im = im * scale
    low = lax.broadcasted_iota(jnp.int32, (F, 2 * NW), 1) < NW
    for pair in range(2):
        lanes = slice(pair * 2 * NW, (pair + 1) * 2 * NW)
        re2, im2 = re[:, lanes], im[:, lanes]
        rows_ref[pl.ds(2 * pair, F, stride=4), :] = jnp.where(low, re2, pltpu.roll(im2, NW, 1))
        rows_ref[pl.ds(2 * pair + 1, F, stride=4), :] = jnp.where(low, pltpu.roll(re2, NW, 1), im2)
    size = HALF * 4
    core = lax.axis_index("row") % N_C
    keep_ref[...] = rows_ref[pl.ds(pl.multiple_of(core * size, size), size), :].astype(jnp.bfloat16)
    send_ref[...] = rows_ref[pl.ds(pl.multiple_of((1 - core) * size, size), size), :].astype(jnp.bfloat16)


def whiten(traces, live_flags, dft, near):
    vmem = pl.BlockSpec(memory_space=pltpu.VMEM)
    smem = pl.BlockSpec(memory_space=pltpu.SMEM)
    shape = pltpu.VMEM((HALF * 4, 2 * NW), jnp.bfloat16)
    return pl.pallas_call(
        whiten_kernel,
        out_shape=(shape, shape),
        in_specs=[smem, vmem, vmem, vmem],
        out_specs=(vmem, vmem),
        scratch_shapes=[pltpu.VMEM((F * 4, 2 * NW), jnp.float32)],
        name="whiten",
    )(live_flags, traces.reshape(4 * NW, SAMP), dft, near)


def merge_kernel(keep_ref, got_ref, out_ref):
    keep = keep_ref[...].astype(jnp.float32).reshape(HALF // 2, 8, 2 * NW)
    got = got_ref[...].astype(jnp.float32).reshape(HALF // 2, 8, 2 * NW)
    first = lax.axis_index("row") % N_C == 0
    a = jnp.where(first, keep, got)
    b = jnp.where(first, got, keep)
    low = lax.broadcasted_iota(jnp.int32, (HALF // 2, 8, 2 * NW), 1) < 4
    even = jnp.where(low, a, pltpu.roll(b, 4, 1))
    odd = jnp.where(low, pltpu.roll(a, 4, 1), b)
    both = jnp.concatenate([even[:, None], odd[:, None]], axis=1)
    out_ref[...] = both.reshape(PIECE, 2 * NW).astype(jnp.bfloat16)


def merge(keep, got):
    vmem = pl.BlockSpec(memory_space=pltpu.VMEM)
    return pl.pallas_call(
        merge_kernel,
        out_shape=pltpu.VMEM((PIECE, 2 * NW), jnp.bfloat16),
        in_specs=[vmem, vmem],
        out_specs=vmem,
        name="merge",
    )(in_vmem(keep), in_vmem(got))


PITCH = 2 * HALF + 8


def placements():
    row, col = lax.axis_index("row"), lax.axis_index("col")
    y, h = row // 4, row // 2 % 2
    x, l = col // N_L, col % N_L
    firsts = []
    for d in (0, -1, 1, 2):
        firsts += [(x + d) % N_X * N_L + (l + q) % N_L for q in (0, 3, 1, 2)]
    spot = lambda d, mine: (y + d) % N_Y * N_H + (h if mine else 1 - h)
    seconds = [spot(0, True), spot(0, False), spot(-1, True), spot(1, True)]
    for d in (1, 2):
        seconds += [spot(-d - 1, True), spot(-d, False), spot(d + 1, True), spot(d, False)]
    seconds += [spot(-4, True), spot(-3, False), spot(3, False), spot(4, False)]
    return row, col, firsts + seconds


def cross_kernel(n_first, *refs):
    firsts, seconds = refs[:n_first], refs[n_first:-5]
    inv_ref, send_ref, own_ref, s_ref, place_ref = refs[-5:]
    row, _, where = placements()
    core = row % N_C
    for slot in range(16):
        place_ref[slot] = where[slot]
    sign = jnp.where(
        lax.broadcasted_iota(jnp.int32, (128, 2 * NW), 1) < NW, 1.0, -1.0
    ).astype(jnp.bfloat16)
    contract = (((1,), (1,)), ((), ()))

    def gather(blocks, f):
        parts = []
        for ref in blocks:
            parts += [ref[f]] if len(ref.shape) == 3 else [ref[n, f] for n in range(ref.shape[0])]
        return jnp.concatenate(parts, axis=0)

    def one_bin(f, carry):
        a = gather(firsts, f)
        b = gather(seconds, f)
        turned = jnp.concatenate([a[:, NW:], a[:, :NW]], axis=1) * sign
        both = jnp.concatenate([a, turned], axis=0)
        terms = lax.dot_general(both, b, contract, preferred_element_type=jnp.float32)
        s_ref[pl.ds(f, 128, stride=PITCH), :] = terms[:128]
        s_ref[pl.ds(f + HALF, 128, stride=PITCH), :] = terms[128:]
        return carry

    lax.fori_loop(0, HALF, one_bin, 0, unroll=UNROLL)

    lane = lax.broadcasted_iota(jnp.int32, (2 * HALF, 128), 1)
    for slot in range(8):
        rows = pl.ds(slot * PITCH, 2 * HALF)
        s_ref[rows, :] = jnp.where(lane == slot, 0.0, s_ref[rows, :])
    table = inv_ref[core]
    spots = row_spots(where)

    def send_step(step, carry):
        piece, half = step // 2, step % 2
        start = pl.multiple_of((piece * 8 + (1 - core) * 4 + half * 2) * PITCH, 8)
        w0 = s_ref[pl.ds(start, 2 * HALF), :].astype(jnp.bfloat16)
        w1 = s_ref[pl.ds(pl.multiple_of(start + PITCH, 8), 2 * HALF), :].astype(jnp.bfloat16)
        store_lags(table, w0, w1, place_ref[piece] * 4 + half * 2, spots, send_ref)
        own = pl.multiple_of((piece * 8 + core * 4 + half * 2) * PITCH, 8)
        at = place_ref[piece] * 4 + half * 2
        own_ref[at] = s_ref[pl.ds(own, 2 * HALF), :].astype(jnp.bfloat16)
        own_ref[at + 1] = s_ref[pl.ds(pl.multiple_of(own + PITCH, 8), 2 * HALF), :].astype(jnp.bfloat16)
        return carry

    lax.fori_loop(0, 32, send_step, 0, unroll=16)


def row_spots(where):
    return [pl.ds(pl.multiple_of(place * 8, 8), 8) for place in where[16:]]


def store_lags(table, w0, w1, i, spots, out_ref):
    lagged = jnp.dot(table, jnp.concatenate([w0, w1], axis=1), preferred_element_type=jnp.float32)
    for n in range(2):
        block = lagged[:, n * 128 : (n + 1) * 128].T
        for slot in range(16):
            out_ref[i + n, spots[slot], :] = block[slot * 8 : slot * 8 + 8].astype(out_ref.dtype)


def lag_kernel(stacked_ref, inv_ref, out_ref):
    row, _, where = placements()
    table = inv_ref[row % N_C]
    spots = row_spots(where)

    def step(pair, carry):
        i = 2 * pair
        store_lags(table, stacked_ref[i], stacked_ref[i + 1], i, spots, out_ref)
        return carry

    lax.fori_loop(0, 32, step, 0, unroll=16)


def lag_own(stacked, inverse):
    vmem = pl.BlockSpec(memory_space=pltpu.VMEM)
    return pl.pallas_call(
        lag_kernel,
        out_shape=pltpu.VMEM((64, 128, LAGS), jnp.float32),
        in_specs=[vmem, vmem],
        out_specs=vmem,
        compiler_params=pltpu.CompilerParams(vmem_limit_bytes=16 * 1024 * 1024),
        cost_estimate=pl.CostEstimate(
            flops=2 * 64 * 128 * LAGS * 2 * HALF, bytes_accessed=1 << 23, transcendentals=0
        ),
        name="lag_own",
    )(in_vmem(stacked), inverse)


def finish_kernel(own_ref, got_ref, out_ref):
    step = out_ref.shape[0]
    rows = pl.ds(pl.multiple_of(pl.program_id(0) * step, step), step)
    out_ref[...] = (own_ref[rows] + got_ref[rows].astype(jnp.float32)).astype(jnp.bfloat16)


def finish(own, got):
    step = 8
    vmem = pl.BlockSpec(memory_space=pltpu.VMEM)
    return pl.pallas_call(
        finish_kernel,
        out_shape=jax.ShapeDtypeStruct((64, 128, LAGS), jnp.bfloat16),
        grid=(64 // step,),
        in_specs=[vmem, vmem],
        out_specs=pl.BlockSpec((step, 128, LAGS), lambda n: (n, 0, 0)),
        compiler_params=pltpu.CompilerParams(vmem_limit_bytes=16 * 1024 * 1024),
        name="finish",
    )(in_vmem(own), in_vmem(got))


UNROLL = 16


def cross(firsts, seconds, inverse):
    kernel = lambda *refs: cross_kernel(len(firsts), *refs)
    vmem = pl.BlockSpec(memory_space=pltpu.VMEM)
    return pl.pallas_call(
        kernel,
        out_shape=(
            pltpu.VMEM((64, 128, LAGS), jnp.bfloat16),
            pltpu.VMEM((64, 2 * HALF, 128), jnp.bfloat16),
        ),
        in_specs=[vmem] * (len(firsts) + len(seconds) + 1),
        out_specs=(vmem, vmem),
        scratch_shapes=[
            pltpu.VMEM((128 * PITCH, 128), jnp.float32),
            pltpu.SMEM((16,), jnp.int32),
        ],
        compiler_params=pltpu.CompilerParams(vmem_limit_bytes=32 * 1024 * 1024),
        name="cross",
    )(*[in_vmem(value) for value in (*firsts, *seconds)], inverse)


def permutation(move):
    pairs = []
    for index in range(N_Y * N_H * N_C * N_X * N_L):
        rest, l = divmod(index, N_L)
        rest, x = divmod(rest, N_X)
        rest, c = divmod(rest, N_C)
        y, h = divmod(rest, N_H)
        y, h, c, x, l = move(y, h, c, x, l)
        pairs.append((index, (((y % N_Y * N_H + h) * N_C + c) * N_X + x % N_X) * N_L + l % N_L))
    return pairs


SWAP_CORE = permutation(lambda y, h, c, x, l: (y, h, 1 - c, x, l))
SWAP_H = permutation(lambda y, h, c, x, l: (y, 1 - h, c, x, l))
STEP_L = [permutation(lambda y, h, c, x, l, d=d: (y, h, c, x, l + d)) for d in range(4)]
Y_UP = permutation(lambda y, h, c, x, l: (y + 1, h, c, x, l))
Y_DOWN = permutation(lambda y, h, c, x, l: (y - 1, h, c, x, l))
X_UP = permutation(lambda y, h, c, x, l: (y, h, c, x + 1, l))
X_DOWN = permutation(lambda y, h, c, x, l: (y, h, c, x - 1, l))


def in_vmem(value):
    return pltpu.with_memory_space_constraint(value, pltpu.VMEM)


def move(value, pairs):
    return lax.ppermute(value, AXES, pairs)


def correlate(traces, live_flags):
    dft, near, inverse = make_tables()
    keep, send = whiten(traces, live_flags, jnp.asarray(dft), jnp.asarray(near))
    piece = merge(keep, move(send, SWAP_CORE)).reshape(HALF, 8, 2 * NW)

    other = move(piece, SWAP_H)
    up1, down1 = move(piece, Y_UP), move(piece, Y_DOWN)
    l1, l3 = move(piece, STEP_L[1]), move(piece, STEP_L[3])
    up2 = move(jnp.stack([up1, other]), Y_UP)
    down2 = move(jnp.stack([down1, other]), Y_DOWN)
    l2 = move(piece, STEP_L[2])
    x1 = jnp.stack([piece, l1])
    x1_up, x1_down = move(x1, X_UP), move(x1, X_DOWN)
    up3, down3 = move(up2, Y_UP), move(down2, Y_DOWN)
    x2 = jnp.stack([l3, l2])
    x2_up, x2_down = move(x2, X_UP), move(x2, X_DOWN)
    x1_far = move(x1_up, X_UP)
    up4 = move(up3, Y_UP)
    down4 = move(down3[1], Y_DOWN)
    x2_far = move(x2_down, X_DOWN)
    down5 = move(down4, Y_DOWN)

    firsts = (x1, x2, x1_up, x2_up, x1_down, x2_down, x1_far, x2_far)
    seconds = (piece, other, up1, down1, up2, down2, up3, down3, up4, down4, down5)
    table = jnp.asarray(inverse)
    sent, stacked = cross(firsts, seconds, table)
    got = move(sent, SWAP_CORE)
    return finish(lag_own(stacked, table), got)


def solution(mesh):
    in_specs = (P(("row", "col"), None, None), P(("row", "col")))
    out_specs = P("row", "col", None)
    return jax.shard_map(
        correlate, mesh=mesh, in_specs=in_specs, out_specs=out_specs, check_vma=False
    )
```

```python
import math

import jax
import jax.numpy as jnp
import numpy as np
from jax import lax
from jax.experimental import pallas as pl
from jax.experimental.pallas import tpu as pltpu
from jax.sharding import PartitionSpec as P

F = 256
LAGS = 128
SAMP = 512
NW = 64
N_Y, N_H, N_C, N_X, N_L = 8, 2, 2, 4, 4
HALF = F // 2
PIECE = HALF * 8
AXES = ("row", "col")


def bf16_parts(table, count):
    parts = []
    rest = table.astype(np.float32)
    for _ in range(count):
        part = rest.astype(jnp.bfloat16)
        parts.append(part)
        rest = rest - part.astype(np.float32)
    return np.stack(parts)


def make_tables():
    samples = np.arange(SAMP)
    bins = np.arange(F)
    angle = 2.0 * math.pi * (bins[:, None] * samples[None, :] % SAMP) / SAMP
    forward = np.concatenate([np.cos(angle), -np.sin(angle)], axis=0)
    taper = 0.5 - 0.5 * np.cos(2.0 * math.pi * samples / SAMP)
    dft = bf16_parts(forward * taper[None, :], 3)
    near = (np.abs(bins[:, None] - bins[None, :]) <= 4).astype(jnp.bfloat16)
    lags = np.arange(LAGS) - LAGS // 2
    langle = 2.0 * math.pi * (bins[:, None] * lags[None, :] % SAMP) / SAMP
    shift = 1.0 / (math.sqrt(NW) * math.sqrt(F))
    cs = np.cos(langle).astype(np.float32).astype(jnp.bfloat16).astype(np.float32)
    sn = np.sin(langle).astype(np.float32).astype(jnp.bfloat16).astype(np.float32)
    inverse = []
    for half in range(2):
        part = slice(half * HALF, (half + 1) * HALF)
        table = np.concatenate([cs[part], -sn[part]], axis=0) * shift
        inverse.append(table.T.astype(jnp.bfloat16))
    return dft, near, np.stack(inverse)


def whiten_kernel(flags_ref, x_ref, dft_ref, near_ref, keep_ref, send_ref, rows_ref):
    x = x_ref[...]
    spectra = None
    for part in (2, 1, 0):
        term = lax.dot_general(
            dft_ref[part], x, (((1,), (1,)), ((), ())), preferred_element_type=jnp.float32
        )
        spectra = term if spectra is None else spectra + term
    re = spectra[:F]
    im = spectra[F:]
    power = re * re + im * im
    bins = lax.broadcasted_iota(jnp.int32, (F, 1), 0)
    counts = jnp.minimum(bins + 4, F - 1) - jnp.maximum(bins - 4, 0) + 1
    high = power.astype(jnp.bfloat16)
    rest = power - high.astype(jnp.float32)
    middle = rest.astype(jnp.bfloat16)
    tail = (rest - middle.astype(jnp.float32)).astype(jnp.bfloat16)
    sums = jnp.dot(
        near_ref[...],
        jnp.concatenate([high, middle, tail], axis=1),
        preferred_element_type=jnp.float32,
    )
    width = power.shape[1]
    total = sums[:, 2 * width :] + sums[:, width : 2 * width] + sums[:, :width]
    smooth = total / counts.astype(jnp.float32)
    level = jnp.mean(power, axis=0, keepdims=True)
    lane = lax.broadcasted_iota(jnp.int32, (1, 4 * NW), 1) // NW
    alive = jnp.zeros((1, 4 * NW), jnp.float32)
    for ch in range(4):
        alive = jnp.where(lane == ch, flags_ref[ch].astype(jnp.float32), alive)
    scale = lax.rsqrt(smooth + 0.05 * level + 1e-06) * alive
    re = re * scale
    im = im * scale
    low = lax.broadcasted_iota(jnp.int32, (F, 2 * NW), 1) < NW
    for pair in range(2):
        lanes = slice(pair * 2 * NW, (pair + 1) * 2 * NW)
        re2, im2 = re[:, lanes], im[:, lanes]
        rows_ref[pl.ds(2 * pair, F, stride=4), :] = jnp.where(low, re2, pltpu.roll(im2, NW, 1))
        rows_ref[pl.ds(2 * pair + 1, F, stride=4), :] = jnp.where(low, pltpu.roll(re2, NW, 1), im2)
    size = HALF * 4
    core = lax.axis_index("row") % N_C
    keep_ref[...] = rows_ref[pl.ds(pl.multiple_of(core * size, size), size), :].astype(jnp.bfloat16)
    send_ref[...] = rows_ref[pl.ds(pl.multiple_of((1 - core) * size, size), size), :].astype(jnp.bfloat16)


def whiten(traces, live_flags, dft, near):
    vmem = pl.BlockSpec(memory_space=pltpu.VMEM)
    smem = pl.BlockSpec(memory_space=pltpu.SMEM)
    shape = pltpu.VMEM((HALF * 4, 2 * NW), jnp.bfloat16)
    return pl.pallas_call(
        whiten_kernel,
        out_shape=(shape, shape),
        in_specs=[smem, vmem, vmem, vmem],
        out_specs=(vmem, vmem),
        scratch_shapes=[pltpu.VMEM((F * 4, 2 * NW), jnp.float32)],
        name="whiten",
    )(live_flags, traces.reshape(4 * NW, SAMP), dft, near)


def merge_kernel(keep_ref, got_ref, out_ref):
    keep = keep_ref[...].astype(jnp.float32).reshape(HALF // 2, 8, 2 * NW)
    got = got_ref[...].astype(jnp.float32).reshape(HALF // 2, 8, 2 * NW)
    first = lax.axis_index("row") % N_C == 0
    a = jnp.where(first, keep, got)
    b = jnp.where(first, got, keep)
    low = lax.broadcasted_iota(jnp.int32, (HALF // 2, 8, 2 * NW), 1) < 4
    even = jnp.where(low, a, pltpu.roll(b, 4, 1))
    odd = jnp.where(low, pltpu.roll(a, 4, 1), b)
    both = jnp.concatenate([even[:, None], odd[:, None]], axis=1)
    out_ref[...] = both.reshape(PIECE, 2 * NW).astype(jnp.bfloat16)


def merge(keep, got):
    vmem = pl.BlockSpec(memory_space=pltpu.VMEM)
    return pl.pallas_call(
        merge_kernel,
        out_shape=pltpu.VMEM((PIECE, 2 * NW), jnp.bfloat16),
        in_specs=[vmem, vmem],
        out_specs=vmem,
        name="merge",
    )(in_vmem(keep), in_vmem(got))


PITCH = 2 * HALF + 8


def placements():
    row, col = lax.axis_index("row"), lax.axis_index("col")
    y, h = row // 4, row // 2 % 2
    x, l = col // N_L, col % N_L
    firsts = []
    for d in (0, -1, 1, 2):
        firsts += [(x + d) % N_X * N_L + (l + q) % N_L for q in (0, 3, 1, 2)]
    spot = lambda d, mine: (y + d) % N_Y * N_H + (h if mine else 1 - h)
    seconds = [spot(0, True), spot(0, False), spot(-1, True), spot(1, True)]
    for d in (1, 2):
        seconds += [spot(-d - 1, True), spot(-d, False), spot(d + 1, True), spot(d, False)]
    seconds += [spot(-4, True), spot(-3, False), spot(3, False), spot(4, False)]
    return row, col, firsts + seconds


def cross_kernel(n_first, *refs):
    firsts, seconds = refs[:n_first], refs[n_first:-5]
    inv_ref, send_ref, own_ref, s_ref, place_ref = refs[-5:]
    row, _, where = placements()
    core = row % N_C
    for slot in range(16):
        place_ref[slot] = where[slot]
    sign = jnp.where(
        lax.broadcasted_iota(jnp.int32, (128, 2 * NW), 1) < NW, 1.0, -1.0
    ).astype(jnp.bfloat16)
    contract = (((1,), (1,)), ((), ()))

    def gather(blocks, f):
        parts = []
        for ref in blocks:
            parts += [ref[f]] if len(ref.shape) == 3 else [ref[n, f] for n in range(ref.shape[0])]
        return jnp.concatenate(parts, axis=0)

    def one_bin(f, carry):
        a = gather(firsts, f)
        b = gather(seconds, f)
        turned = jnp.concatenate([a[:, NW:], a[:, :NW]], axis=1) * sign
        both = jnp.concatenate([a, turned], axis=0)
        terms = lax.dot_general(both, b, contract, preferred_element_type=jnp.float32)
        s_ref[pl.ds(f, 128, stride=PITCH), :] = terms[:128]
        s_ref[pl.ds(f + HALF, 128, stride=PITCH), :] = terms[128:]
        return carry

    lax.fori_loop(0, HALF, one_bin, 0, unroll=UNROLL)

    lane = lax.broadcasted_iota(jnp.int32, (2 * HALF, 128), 1)
    for slot in range(8):
        rows = pl.ds(slot * PITCH, 2 * HALF)
        s_ref[rows, :] = jnp.where(lane == slot, 0.0, s_ref[rows, :])
    table = inv_ref[core]
    spots = row_spots(where)

    def send_step(step, carry):
        piece, half = step // 2, step % 2
        start = pl.multiple_of((piece * 8 + (1 - core) * 4 + half * 2) * PITCH, 8)
        w0 = s_ref[pl.ds(start, 2 * HALF), :].astype(jnp.bfloat16)
        w1 = s_ref[pl.ds(pl.multiple_of(start + PITCH, 8), 2 * HALF), :].astype(jnp.bfloat16)
        store_lags(table, w0, w1, place_ref[piece] * 4 + half * 2, spots, send_ref)
        own = pl.multiple_of((piece * 8 + core * 4 + half * 2) * PITCH, 8)
        at = place_ref[piece] * 4 + half * 2
        own_ref[at] = s_ref[pl.ds(own, 2 * HALF), :].astype(jnp.bfloat16)
        own_ref[at + 1] = s_ref[pl.ds(pl.multiple_of(own + PITCH, 8), 2 * HALF), :].astype(jnp.bfloat16)
        return carry

    lax.fori_loop(0, 32, send_step, 0, unroll=16)


def row_spots(where):
    return [pl.ds(pl.multiple_of(place * 8, 8), 8) for place in where[16:]]


def store_lags(table, w0, w1, i, spots, out_ref):
    lagged = jnp.dot(table, jnp.concatenate([w0, w1], axis=1), preferred_element_type=jnp.float32)
    for n in range(2):
        block = lagged[:, n * 128 : (n + 1) * 128].T
        for slot in range(16):
            out_ref[i + n, spots[slot], :] = block[slot * 8 : slot * 8 + 8].astype(out_ref.dtype)


def lag_kernel(stacked_ref, inv_ref, out_ref):
    row, _, where = placements()
    table = inv_ref[row % N_C]
    spots = row_spots(where)

    def step(pair, carry):
        i = 2 * pair
        store_lags(table, stacked_ref[i], stacked_ref[i + 1], i, spots, out_ref)
        return carry

    lax.fori_loop(0, 32, step, 0, unroll=16)


def lag_own(stacked, inverse):
    vmem = pl.BlockSpec(memory_space=pltpu.VMEM)
    return pl.pallas_call(
        lag_kernel,
        out_shape=pltpu.VMEM((64, 128, LAGS), jnp.float32),
        in_specs=[vmem, vmem],
        out_specs=vmem,
        compiler_params=pltpu.CompilerParams(vmem_limit_bytes=16 * 1024 * 1024),
        cost_estimate=pl.CostEstimate(
            flops=2 * 64 * 128 * LAGS * 2 * HALF, bytes_accessed=1 << 23, transcendentals=0
        ),
        name="lag_own",
    )(in_vmem(stacked), inverse)


def finish_kernel(own_ref, got_ref, out_ref):
    step = out_ref.shape[0]
    rows = pl.ds(pl.multiple_of(pl.program_id(0) * step, step), step)
    out_ref[...] = (own_ref[rows] + got_ref[rows].astype(jnp.float32)).astype(jnp.bfloat16)


def finish(own, got):
    step = 8
    vmem = pl.BlockSpec(memory_space=pltpu.VMEM)
    return pl.pallas_call(
        finish_kernel,
        out_shape=jax.ShapeDtypeStruct((64, 128, LAGS), jnp.bfloat16),
        grid=(64 // step,),
        in_specs=[vmem, vmem],
        out_specs=pl.BlockSpec((step, 128, LAGS), lambda n: (n, 0, 0)),
        compiler_params=pltpu.CompilerParams(vmem_limit_bytes=16 * 1024 * 1024),
        name="finish",
    )(in_vmem(own), in_vmem(got))


UNROLL = 16


def cross(firsts, seconds, inverse):
    kernel = lambda *refs: cross_kernel(len(firsts), *refs)
    vmem = pl.BlockSpec(memory_space=pltpu.VMEM)
    return pl.pallas_call(
        kernel,
        out_shape=(
            pltpu.VMEM((64, 128, LAGS), jnp.bfloat16),
            pltpu.VMEM((64, 2 * HALF, 128), jnp.bfloat16),
        ),
        in_specs=[vmem] * (len(firsts) + len(seconds) + 1),
        out_specs=(vmem, vmem),
        scratch_shapes=[
            pltpu.VMEM((128 * PITCH, 128), jnp.float32),
            pltpu.SMEM((16,), jnp.int32),
        ],
        compiler_params=pltpu.CompilerParams(vmem_limit_bytes=32 * 1024 * 1024),
        name="cross",
    )(*[in_vmem(value) for value in (*firsts, *seconds)], inverse)


def permutation(move):
    pairs = []
    for index in range(N_Y * N_H * N_C * N_X * N_L):
        rest, l = divmod(index, N_L)
        rest, x = divmod(rest, N_X)
        rest, c = divmod(rest, N_C)
        y, h = divmod(rest, N_H)
        y, h, c, x, l = move(y, h, c, x, l)
        pairs.append((index, (((y % N_Y * N_H + h) * N_C + c) * N_X + x % N_X) * N_L + l % N_L))
    return pairs


SWAP_CORE = permutation(lambda y, h, c, x, l: (y, h, 1 - c, x, l))
SWAP_H = permutation(lambda y, h, c, x, l: (y, 1 - h, c, x, l))
STEP_L = [permutation(lambda y, h, c, x, l, d=d: (y, h, c, x, l + d)) for d in range(4)]
Y_UP = permutation(lambda y, h, c, x, l: (y + 1, h, c, x, l))
Y_DOWN = permutation(lambda y, h, c, x, l: (y - 1, h, c, x, l))
Y_DOWN2 = permutation(lambda y, h, c, x, l: (y - 2, h, c, x, l))
X_UP = permutation(lambda y, h, c, x, l: (y, h, c, x + 1, l))
X_DOWN = permutation(lambda y, h, c, x, l: (y, h, c, x - 1, l))


def in_vmem(value):
    return pltpu.with_memory_space_constraint(value, pltpu.VMEM)


def move(value, pairs):
    return lax.ppermute(value, AXES, pairs)


def correlate(traces, live_flags):
    dft, near, inverse = make_tables()
    keep, send = whiten(traces, live_flags, jnp.asarray(dft), jnp.asarray(near))
    piece = merge(keep, move(send, SWAP_CORE)).reshape(HALF, 8, 2 * NW)

    other = move(piece, SWAP_H)
    up1, down1 = move(piece, Y_UP), move(piece, Y_DOWN)
    l1, l3 = move(piece, STEP_L[1]), move(piece, STEP_L[3])
    up2 = move(jnp.stack([up1, other]), Y_UP)
    down2 = move(jnp.stack([down1, other]), Y_DOWN)
    l2 = move(piece, STEP_L[2])
    x1 = jnp.stack([piece, l1])
    x1_up, x1_down = move(x1, X_UP), move(x1, X_DOWN)
    up3, down3 = move(up2, Y_UP), move(down2, Y_DOWN)
    x2 = jnp.stack([l3, l2])
    x2_up, x2_down = move(x2, X_UP), move(x2, X_DOWN)
    x1_far = move(x1_up, X_UP)
    up4 = move(up3, Y_UP)
    far = down3[1]
    down4 = move(far, Y_DOWN)
    x2_far = move(x2_down, X_DOWN)
    down5 = move(far, Y_DOWN2)

    firsts = (x1, x2, x1_up, x2_up, x1_down, x2_down, x1_far, x2_far)
    seconds = (piece, other, up1, down1, up2, down2, up3, down3, up4, down4, down5)
    table = jnp.asarray(inverse)
    sent, stacked = cross(firsts, seconds, table)
    got = move(sent, SWAP_CORE)
    return finish(lag_own(stacked, table), got)


def solution(mesh):
    in_specs = (P(("row", "col"), None, None), P(("row", "col")))
    out_specs = P("row", "col", None)
    return jax.shard_map(
        correlate, mesh=mesh, in_specs=in_specs, out_specs=out_specs, check_vma=False
    )
```

```python
import math

import jax
import jax.numpy as jnp
import numpy as np
from jax import lax
from jax.experimental import pallas as pl
from jax.experimental.pallas import tpu as pltpu
from jax.sharding import PartitionSpec as P

F = 256
LAGS = 128
SAMP = 512
NW = 64
N_Y, N_H, N_C, N_X, N_L = 8, 2, 2, 4, 4
HALF = F // 2
PIECE = HALF * 8
AXES = ("row", "col")


def bf16_parts(table, count):
    parts = []
    rest = table.astype(np.float32)
    for _ in range(count):
        part = rest.astype(jnp.bfloat16)
        parts.append(part)
        rest = rest - part.astype(np.float32)
    return np.stack(parts)


def make_tables():
    samples = np.arange(SAMP)
    bins = np.arange(F)
    angle = 2.0 * math.pi * (bins[:, None] * samples[None, :] % SAMP) / SAMP
    forward = np.concatenate([np.cos(angle), -np.sin(angle)], axis=0)
    taper = 0.5 - 0.5 * np.cos(2.0 * math.pi * samples / SAMP)
    dft = bf16_parts(forward * taper[None, :], 3)
    near = (np.abs(bins[:, None] - bins[None, :]) <= 4).astype(jnp.bfloat16)
    lags = np.arange(LAGS) - LAGS // 2
    langle = 2.0 * math.pi * (bins[:, None] * lags[None, :] % SAMP) / SAMP
    shift = 1.0 / (math.sqrt(NW) * math.sqrt(F))
    cs = np.cos(langle).astype(np.float32).astype(jnp.bfloat16).astype(np.float32)
    sn = np.sin(langle).astype(np.float32).astype(jnp.bfloat16).astype(np.float32)
    inverse = []
    for half in range(2):
        part = slice(half * HALF, (half + 1) * HALF)
        table = np.concatenate([cs[part], -sn[part]], axis=0) * shift
        inverse.append(table.T.astype(jnp.bfloat16))
    return dft, near, np.stack(inverse)


def whiten_kernel(flags_ref, x_ref, dft_ref, near_ref, keep_ref, send_ref, rows_ref):
    x = x_ref[...]
    spectra = None
    for part in (2, 1, 0):
        term = lax.dot_general(
            dft_ref[part], x, (((1,), (1,)), ((), ())), preferred_element_type=jnp.float32
        )
        spectra = term if spectra is None else spectra + term
    re = spectra[:F]
    im = spectra[F:]
    power = re * re + im * im
    bins = lax.broadcasted_iota(jnp.int32, (F, 1), 0)
    counts = jnp.minimum(bins + 4, F - 1) - jnp.maximum(bins - 4, 0) + 1
    high = power.astype(jnp.bfloat16)
    rest = power - high.astype(jnp.float32)
    middle = rest.astype(jnp.bfloat16)
    tail = (rest - middle.astype(jnp.float32)).astype(jnp.bfloat16)
    sums = jnp.dot(
        near_ref[...],
        jnp.concatenate([high, middle, tail], axis=1),
        preferred_element_type=jnp.float32,
    )
    width = power.shape[1]
    total = sums[:, 2 * width :] + sums[:, width : 2 * width] + sums[:, :width]
    smooth = total / counts.astype(jnp.float32)
    level = jnp.mean(power, axis=0, keepdims=True)
    lane = lax.broadcasted_iota(jnp.int32, (1, 4 * NW), 1) // NW
    alive = jnp.zeros((1, 4 * NW), jnp.float32)
    for ch in range(4):
        alive = jnp.where(lane == ch, flags_ref[ch].astype(jnp.float32), alive)
    scale = lax.rsqrt(smooth + 0.05 * level + 1e-06) * alive
    re = re * scale
    im = im * scale
    low = lax.broadcasted_iota(jnp.int32, (F, 2 * NW), 1) < NW
    for pair in range(2):
        lanes = slice(pair * 2 * NW, (pair + 1) * 2 * NW)
        re2, im2 = re[:, lanes], im[:, lanes]
        rows_ref[pl.ds(2 * pair, F, stride=4), :] = jnp.where(low, re2, pltpu.roll(im2, NW, 1))
        rows_ref[pl.ds(2 * pair + 1, F, stride=4), :] = jnp.where(low, pltpu.roll(re2, NW, 1), im2)
    size = HALF * 4
    core = lax.axis_index("row") % N_C
    keep_ref[...] = rows_ref[pl.ds(pl.multiple_of(core * size, size), size), :].astype(jnp.bfloat16)
    send_ref[...] = rows_ref[pl.ds(pl.multiple_of((1 - core) * size, size), size), :].astype(jnp.bfloat16)


def whiten(traces, live_flags, dft, near):
    vmem = pl.BlockSpec(memory_space=pltpu.VMEM)
    smem = pl.BlockSpec(memory_space=pltpu.SMEM)
    shape = pltpu.VMEM((HALF * 4, 2 * NW), jnp.bfloat16)
    return pl.pallas_call(
        whiten_kernel,
        out_shape=(shape, shape),
        in_specs=[smem, vmem, vmem, vmem],
        out_specs=(vmem, vmem),
        scratch_shapes=[pltpu.VMEM((F * 4, 2 * NW), jnp.float32)],
        name="whiten",
    )(live_flags, traces.reshape(4 * NW, SAMP), dft, near)


def merge_kernel(keep_ref, got_ref, out_ref):
    keep = keep_ref[...].astype(jnp.float32).reshape(HALF // 2, 8, 2 * NW)
    got = got_ref[...].astype(jnp.float32).reshape(HALF // 2, 8, 2 * NW)
    first = lax.axis_index("row") % N_C == 0
    a = jnp.where(first, keep, got)
    b = jnp.where(first, got, keep)
    low = lax.broadcasted_iota(jnp.int32, (HALF // 2, 8, 2 * NW), 1) < 4
    even = jnp.where(low, a, pltpu.roll(b, 4, 1))
    odd = jnp.where(low, pltpu.roll(a, 4, 1), b)
    both = jnp.concatenate([even[:, None], odd[:, None]], axis=1)
    out_ref[...] = both.reshape(PIECE, 2 * NW).astype(jnp.bfloat16)


def merge(keep, got):
    vmem = pl.BlockSpec(memory_space=pltpu.VMEM)
    return pl.pallas_call(
        merge_kernel,
        out_shape=pltpu.VMEM((PIECE, 2 * NW), jnp.bfloat16),
        in_specs=[vmem, vmem],
        out_specs=vmem,
        name="merge",
    )(in_vmem(keep), in_vmem(got))


PITCH = 2 * HALF + 8


def placements():
    row, col = lax.axis_index("row"), lax.axis_index("col")
    y, h = row // 4, row // 2 % 2
    x, l = col // N_L, col % N_L
    firsts = []
    for d in (0, -1, 1, 2):
        firsts += [(x + d) % N_X * N_L + (l + q) % N_L for q in (0, 3, 1, 2)]
    spot = lambda d, mine: (y + d) % N_Y * N_H + (h if mine else 1 - h)
    seconds = [spot(0, True), spot(0, False), spot(-1, True), spot(1, True)]
    for d in (1, 2):
        seconds += [spot(-d - 1, True), spot(-d, False), spot(d + 1, True), spot(d, False)]
    seconds += [spot(-4, True), spot(-3, False), spot(3, False), spot(4, False)]
    return row, col, firsts + seconds


def cross_kernel(n_first, *refs):
    firsts, seconds = refs[:n_first], refs[n_first:-5]
    inv_ref, send_ref, own_ref, s_ref, place_ref = refs[-5:]
    row, _, where = placements()
    core = row % N_C
    for slot in range(16):
        place_ref[slot] = where[slot]
    sign = jnp.where(
        lax.broadcasted_iota(jnp.int32, (128, 2 * NW), 1) < NW, 1.0, -1.0
    ).astype(jnp.bfloat16)
    contract = (((1,), (1,)), ((), ()))

    def gather(blocks, f):
        parts = []
        for ref in blocks:
            parts += [ref[f]] if len(ref.shape) == 3 else [ref[n, f] for n in range(ref.shape[0])]
        return jnp.concatenate(parts, axis=0)

    def one_bin(f, carry):
        a = gather(firsts, f)
        b = gather(seconds, f)
        turned = jnp.concatenate([a[:, NW:], a[:, :NW]], axis=1) * sign
        both = jnp.concatenate([a, turned], axis=0)
        terms = lax.dot_general(both, b, contract, preferred_element_type=jnp.float32)
        s_ref[pl.ds(f, 128, stride=PITCH), :] = terms[:128]
        s_ref[pl.ds(f + HALF, 128, stride=PITCH), :] = terms[128:]
        return carry

    lax.fori_loop(0, HALF, one_bin, 0, unroll=UNROLL)

    lane = lax.broadcasted_iota(jnp.int32, (2 * HALF, 128), 1)
    for slot in range(8):
        rows = pl.ds(slot * PITCH, 2 * HALF)
        s_ref[rows, :] = jnp.where(lane == slot, 0.0, s_ref[rows, :])
    table = inv_ref[core]
    spots = row_spots(where)

    def send_step(step, carry):
        piece, half = step // 2, step % 2
        start = pl.multiple_of((piece * 8 + (1 - core) * 4 + half * 2) * PITCH, 8)
        w0 = s_ref[pl.ds(start, 2 * HALF), :].astype(jnp.bfloat16)
        w1 = s_ref[pl.ds(pl.multiple_of(start + PITCH, 8), 2 * HALF), :].astype(jnp.bfloat16)
        store_lags(table, w0, w1, place_ref[piece] * 4 + half * 2, spots, send_ref)
        own = pl.multiple_of((piece * 8 + core * 4 + half * 2) * PITCH, 8)
        at = place_ref[piece] * 4 + half * 2
        own_ref[at] = s_ref[pl.ds(own, 2 * HALF), :].astype(jnp.bfloat16)
        own_ref[at + 1] = s_ref[pl.ds(pl.multiple_of(own + PITCH, 8), 2 * HALF), :].astype(jnp.bfloat16)
        return carry

    lax.fori_loop(0, 32, send_step, 0, unroll=16)


def row_spots(where):
    return [pl.ds(pl.multiple_of(place * 8, 8), 8) for place in where[16:]]


def store_lags(table, w0, w1, i, spots, out_ref):
    lagged = jnp.dot(table, jnp.concatenate([w0, w1], axis=1), preferred_element_type=jnp.float32)
    for n in range(2):
        block = lagged[:, n * 128 : (n + 1) * 128].T
        for slot in range(16):
            out_ref[i + n, spots[slot], :] = block[slot * 8 : slot * 8 + 8].astype(out_ref.dtype)


def lag_kernel(stacked_ref, inv_ref, out_ref):
    row, _, where = placements()
    table = inv_ref[row % N_C]
    spots = row_spots(where)

    def step(pair, carry):
        i = 2 * pair
        store_lags(table, stacked_ref[i], stacked_ref[i + 1], i, spots, out_ref)
        return carry

    lax.fori_loop(0, 32, step, 0, unroll=16)


def lag_own(stacked, inverse):
    vmem = pl.BlockSpec(memory_space=pltpu.VMEM)
    return pl.pallas_call(
        lag_kernel,
        out_shape=pltpu.VMEM((64, 128, LAGS), jnp.float32),
        in_specs=[vmem, vmem],
        out_specs=vmem,
        compiler_params=pltpu.CompilerParams(vmem_limit_bytes=16 * 1024 * 1024),
        cost_estimate=pl.CostEstimate(
            flops=2 * 64 * 128 * LAGS * 2 * HALF, bytes_accessed=1 << 23, transcendentals=0
        ),
        name="lag_own",
    )(in_vmem(stacked), inverse)


UNROLL = 16


def cross(firsts, seconds, inverse):
    kernel = lambda *refs: cross_kernel(len(firsts), *refs)
    vmem = pl.BlockSpec(memory_space=pltpu.VMEM)
    return pl.pallas_call(
        kernel,
        out_shape=(
            pltpu.VMEM((64, 128, LAGS), jnp.bfloat16),
            pltpu.VMEM((64, 2 * HALF, 128), jnp.bfloat16),
        ),
        in_specs=[vmem] * (len(firsts) + len(seconds) + 1),
        out_specs=(vmem, vmem),
        scratch_shapes=[
            pltpu.VMEM((128 * PITCH, 128), jnp.float32),
            pltpu.SMEM((16,), jnp.int32),
        ],
        compiler_params=pltpu.CompilerParams(vmem_limit_bytes=32 * 1024 * 1024),
        name="cross",
    )(*[in_vmem(value) for value in (*firsts, *seconds)], inverse)


def permutation(move):
    pairs = []
    for index in range(N_Y * N_H * N_C * N_X * N_L):
        rest, l = divmod(index, N_L)
        rest, x = divmod(rest, N_X)
        rest, c = divmod(rest, N_C)
        y, h = divmod(rest, N_H)
        y, h, c, x, l = move(y, h, c, x, l)
        pairs.append((index, (((y % N_Y * N_H + h) * N_C + c) * N_X + x % N_X) * N_L + l % N_L))
    return pairs


SWAP_CORE = permutation(lambda y, h, c, x, l: (y, h, 1 - c, x, l))
SWAP_H = permutation(lambda y, h, c, x, l: (y, 1 - h, c, x, l))
STEP_L = [permutation(lambda y, h, c, x, l, d=d: (y, h, c, x, l + d)) for d in range(4)]
Y_UP = permutation(lambda y, h, c, x, l: (y + 1, h, c, x, l))
Y_DOWN = permutation(lambda y, h, c, x, l: (y - 1, h, c, x, l))
X_UP = permutation(lambda y, h, c, x, l: (y, h, c, x + 1, l))
X_DOWN = permutation(lambda y, h, c, x, l: (y, h, c, x - 1, l))


def in_vmem(value):
    return pltpu.with_memory_space_constraint(value, pltpu.VMEM)


def move(value, pairs):
    return lax.ppermute(value, AXES, pairs)


def correlate(traces, live_flags):
    dft, near, inverse = make_tables()
    keep, send = whiten(traces, live_flags, jnp.asarray(dft), jnp.asarray(near))
    piece = merge(keep, move(send, SWAP_CORE)).reshape(HALF, 8, 2 * NW)

    other = move(piece, SWAP_H)
    up1, down1 = move(piece, Y_UP), move(piece, Y_DOWN)
    l1, l3 = move(piece, STEP_L[1]), move(piece, STEP_L[3])
    up2 = move(jnp.stack([up1, other]), Y_UP)
    down2 = move(jnp.stack([down1, other]), Y_DOWN)
    l2 = move(piece, STEP_L[2])
    x1 = jnp.stack([piece, l1])
    x1_up, x1_down = move(x1, X_UP), move(x1, X_DOWN)
    up3, down3 = move(up2, Y_UP), move(down2, Y_DOWN)
    x2 = jnp.stack([l3, l2])
    x2_up, x2_down = move(x2, X_UP), move(x2, X_DOWN)
    x1_far = move(x1_up, X_UP)
    up4 = move(up3, Y_UP)
    down4 = move(down3[1], Y_DOWN)
    x2_far = move(x2_down, X_DOWN)
    down5 = move(down4, Y_DOWN)

    firsts = (x1, x2, x1_up, x2_up, x1_down, x2_down, x1_far, x2_far)
    seconds = (piece, other, up1, down1, up2, down2, up3, down3, up4, down4, down5)
    table = jnp.asarray(inverse)
    sent, stacked = cross(firsts, seconds, table)
    got = move(sent, SWAP_CORE)
    own = lag_own(stacked, table)
    return (own + got.astype(jnp.float32)).astype(jnp.bfloat16)


def solution(mesh):
    in_specs = (P(("row", "col"), None, None), P(("row", "col")))
    out_specs = P("row", "col", None)
    return jax.shard_map(
        correlate, mesh=mesh, in_specs=in_specs, out_specs=out_specs, check_vma=False
    )
```
